32 devices in a mesh: dp: 8 (over z, core), seq: 4 (over y, x).
Axes of the slice: x: 2, y: 2, z: 4, core: 2. Of those that a mesh axis runs over, the one named last changes fastest.
Arguments:
- gated_part: bfloat16 [8, 3072, 4096], P('dp', 'seq'), may hold values from -6 to 6
- mixed_part: bfloat16 [8, 3072, 4096], P('dp', 'seq'), may hold values from -400 to 400
- out_grad: bfloat16 [8, 3072, 4096], P('dp', 'seq'), may hold values from -6 to 6
- norm_gain: float32 [4096], replicated, may hold values from 0.1 to 1.9
- mix_bias: float32 [3072], replicated, may hold values from -4 to 4
- token_mixing_weight: bfloat16 [18, 128, 128], replicated, may hold values from -0.125 to 0.125
- stride_cols: int32 [24, 2], replicated, may hold values from -1 to 7, as said below
Outputs:
- gated_grad: bfloat16 [8, 3072, 4096], P('dp', 'seq')
- value_grad: bfloat16 [8, 3072, 4096], P('dp', 'seq')
- weight_grad: float32 [18, 128, 128], replicated
- gain_grad: float32 [4096], replicated
- bias_grad: float32 [3072], P('seq')
The draws below stay inside these ranges and needn't reach their ends.
Inputs may be any that keep to these rules, and one draw needn't show every extreme that they name: stride_cols[i, s] is -1 for row blocks i < 16, and otherwise a column block from 0 to i - 16; -1 means no strided block; stride_cols[23, 0] is 7.
All inputs are finite; a program needn't handle non-finite values.
Results may differ from the reference program's by a relative error of at most 0.0085.
Values may be sent and summed in bfloat16 or wider, within the bound.
No kernel may reach another device: no remote copies, remote signals or barrier semaphores. Data moves between devices by JAX's collectives and lax.ppermute only.
A program may use at most 320 MiB of HBM per device.

```python
import math
import jax
import jax.numpy as jnp
from jax import lax

HALF_FEATURES = 4096
SEQUENCE_LENGTH = 3072
MIXING_BLOCK = 128
BAND_BLOCKS = 16
NSTR = 2
BATCH = 8
NB = 24
WEIGHT_SLOTS = 18


def draw_mixed_part(key, part):
    key_base, key_rows, key_cols = jax.random.split(key, 3)
    full_shape = (BATCH, SEQUENCE_LENGTH, HALF_FEATURES)
    base_draw = jax.random.normal(key_base, full_shape, jnp.float32)
    base_draw = jnp.clip(base_draw, -4.0, 4.0)
    row_scale = jnp.exp(jax.random.uniform(key_rows, (BATCH, SEQUENCE_LENGTH, 1), jnp.float32, 0.0, math.log(10.0)))
    col_scale = jnp.exp(jax.random.uniform(key_cols, (1, 1, HALF_FEATURES), jnp.float32, 0.0, math.log(10.0)))
    return (base_draw * row_scale * col_scale).astype(jnp.bfloat16)


def draw_stride_cols(key, part):
    row_idx = jnp.arange(NB, dtype=jnp.int32)[:, None]
    slot_idx = jnp.arange(NSTR, dtype=jnp.int32)[None, :]
    pick_span = jnp.maximum(row_idx - BAND_BLOCKS + 1, 1)
    raw_pick = jax.random.randint(key, (NB, NSTR), 0, 1 << 20, dtype=jnp.int32)
    chosen = raw_pick % pick_span
    chosen = jnp.where((row_idx == NB - 1) & (slot_idx == 0), pick_span - 1, chosen)
    return jnp.where(row_idx >= BAND_BLOCKS, chosen, -1).astype(jnp.int32)


def level_of(own_key, extent, shards, smallest, largest):
    loudness = 1.0
    for dim, parts in shards:
        draws = jax.random.uniform(jax.random.fold_in(jax.random.fold_in(own_key, 6), dim), (parts,), jnp.float32, smallest / len(shards), largest / len(shards))
        loudness = loudness * jnp.repeat(jnp.exp(draws), extent[dim] // parts).reshape((-1,) + (1,) * (len(extent) - 1 - dim))
    return loudness


def normal_values(own_key, extent, spread, most, cuts=(), kind=jnp.bfloat16):
    array = jax.random.normal(own_key, extent, jnp.float32) * spread
    if len(cuts) > 0:
        array = level_of(own_key, extent, cuts, -0.22, 0.18) * array
    return jnp.clip(array, min=-most, max=most).astype(kind)


def setup_inputs(seed: int = 0) -> dict:
    key_list = jax.random.split(jax.random.key(seed), 8)
    gated_part = normal_values(key_list[0], (BATCH, SEQUENCE_LENGTH, HALF_FEATURES), 1.0, 6.0, ((0, 8), (1, 4)))
    mixed_part = draw_mixed_part(jax.random.fold_in(key_list[7], 71), 0)
    out_grad = normal_values(key_list[2], (BATCH, SEQUENCE_LENGTH, HALF_FEATURES), 1.0, 6.0, ((0, 8), (1, 4)))
    norm_gain = jnp.clip(1.0 + 0.18 * jax.random.normal(key_list[3], (HALF_FEATURES,), jnp.float32), 0.1, 1.9)
    mix_bias = normal_values(key_list[4], (SEQUENCE_LENGTH,), 1.0, 4.0, (), jnp.float32)
    token_mixing_weight = normal_values(key_list[5], (WEIGHT_SLOTS, MIXING_BLOCK, MIXING_BLOCK), (MIXING_BLOCK * BAND_BLOCKS) ** -0.5, 0.125)
    stride_cols = draw_stride_cols(jax.random.fold_in(key_list[7], 71), 0)
    return {"gated_part": gated_part, "mixed_part": mixed_part, "out_grad": out_grad, "norm_gain": norm_gain, "mix_bias": mix_bias, "token_mixing_weight": token_mixing_weight, "stride_cols": stride_cols}


EPS = 1e-05

def slot_mask(shape):
    slot_idx = lax.broadcasted_iota(jnp.int32, shape, 0)
    row_idx = lax.broadcasted_iota(jnp.int32, shape, 1)
    col_idx = lax.broadcasted_iota(jnp.int32, shape, 2)
    return (slot_idx > 0) | (row_idx >= col_idx)

def shift_down(blocks, offset):
    zero_pad = jnp.zeros((offset,) + blocks.shape[1:], blocks.dtype)
    return jnp.concatenate([zero_pad, blocks[:blocks.shape[0] - offset]], axis=0)

def shift_up(blocks, offset):
    zero_pad = jnp.zeros((offset,) + blocks.shape[1:], blocks.dtype)
    return jnp.concatenate([blocks[offset:], zero_pad], axis=0)

def reference(gated_part, mixed_part, out_grad, norm_gain, mix_bias, token_mixing_weight, stride_cols):
    keep_mask = slot_mask(token_mixing_weight.shape)
    weights = jnp.where(keep_mask, token_mixing_weight.astype(jnp.float32), jnp.zeros((), jnp.float32))
    valid_rows = stride_cols >= 0
    safe_cols = jnp.maximum(stride_cols, 0).astype(jnp.int32)

    def one_sequence(carry, inputs):
        weight_acc, gain_acc, bias_acc = carry
        gated_seq, value_seq, grad_seq = inputs
        values = value_seq.astype(jnp.float32)
        row_mean = lax.optimization_barrier(jnp.mean(values, axis=1, keepdims=True))
        centered = values - row_mean
        row_var = lax.optimization_barrier(jnp.mean(centered * centered, axis=1, keepdims=True))
        inv_std = lax.rsqrt(row_var + EPS)
        norm_hat = centered * inv_std
        normed = (norm_hat * norm_gain).astype(jnp.bfloat16)
        blocks = normed.astype(jnp.float32).reshape(NB, MIXING_BLOCK, HALF_FEATURES)
        mixed_sum = jnp.zeros((NB, MIXING_BLOCK, HALF_FEATURES), jnp.float32)
        for offset in range(BAND_BLOCKS):
            mixed_sum = mixed_sum + jnp.einsum('ab,nbc->nac', weights[offset], shift_down(blocks, offset))
        picked_all = []
        for strided in range(NSTR):
            picked = jnp.where(valid_rows[:, strided, None, None], blocks[safe_cols[:, strided]], jnp.zeros((), jnp.float32))
            picked_all.append(picked)
            mixed_sum = mixed_sum + jnp.einsum('ab,nbc->nac', weights[BAND_BLOCKS + strided], picked)
        mixed_sum = mixed_sum.reshape(SEQUENCE_LENGTH, HALF_FEATURES) + mix_bias[:, None]
        mixed16 = mixed_sum.astype(jnp.bfloat16)
        grad_f32 = grad_seq.astype(jnp.float32)
        gated_grad = (grad_f32 * mixed16.astype(jnp.float32)).astype(jnp.bfloat16)
        dmix16 = (grad_f32 * gated_seq.astype(jnp.float32)).astype(jnp.bfloat16)
        bias_part = lax.optimization_barrier(jnp.sum(dmix16.astype(jnp.float32), axis=1))
        dblocks = dmix16.astype(jnp.float32).reshape(NB, MIXING_BLOCK, HALF_FEATURES)
        dnorm = jnp.zeros((NB, MIXING_BLOCK, HALF_FEATURES), jnp.float32)
        slot_grads = []
        for offset in range(BAND_BLOCKS):
            dnorm = dnorm + jnp.einsum('ab,nac->nbc', weights[offset], shift_up(dblocks, offset))
            slot_grads.append(jnp.einsum('nac,nbc->ab', dblocks, shift_down(blocks, offset)))
        for strided in range(NSTR):
            slot_grads.append(jnp.einsum('nac,nbc->ab', dblocks, picked_all[strided]))
            scatter_term = jnp.einsum('ab,nac->nbc', weights[BAND_BLOCKS + strided], dblocks)
            scatter_term = jnp.where(valid_rows[:, strided, None, None], scatter_term, jnp.zeros((), jnp.float32))
            dnorm = dnorm.at[safe_cols[:, strided]].add(scatter_term)
        slot_grad = jnp.where(keep_mask, jnp.stack(slot_grads), jnp.zeros((), jnp.float32))
        dnorm16 = dnorm.reshape(SEQUENCE_LENGTH, HALF_FEATURES).astype(jnp.bfloat16)
        dnorm_f32 = dnorm16.astype(jnp.float32)
        hat_grad = dnorm_f32 * norm_gain
        value_grad = inv_std * (hat_grad - lax.optimization_barrier(jnp.mean(hat_grad, axis=1, keepdims=True)) - norm_hat * lax.optimization_barrier(jnp.mean(hat_grad * norm_hat, axis=1, keepdims=True)))
        gain_part = lax.optimization_barrier(jnp.sum(dnorm_f32 * norm_hat, axis=0))
        new_carry = (weight_acc + slot_grad, gain_acc + gain_part, bias_acc + bias_part)
        return (new_carry, (gated_grad, value_grad.astype(jnp.bfloat16)))
    initialize = (jnp.zeros((WEIGHT_SLOTS, MIXING_BLOCK, MIXING_BLOCK), jnp.float32), jnp.zeros((HALF_FEATURES,), jnp.float32), jnp.zeros((SEQUENCE_LENGTH,), jnp.float32))
    carry, outputs = lax.scan(one_sequence, initialize, (gated_part, mixed_part, out_grad))
    weight_acc, gain_acc, bias_acc = carry
    gated_grad, value_grad = outputs
    weight_grad = weight_acc / math.sqrt(BATCH * SEQUENCE_LENGTH * HALF_FEATURES)
    gain_grad = gain_acc / math.sqrt(BATCH * SEQUENCE_LENGTH)
    bias_grad = bias_acc / math.sqrt(BATCH * HALF_FEATURES)
    return (gated_grad, value_grad, weight_grad, gain_grad, bias_grad)
```

```python
import math

import jax
import jax.numpy as jnp
from jax import lax
from jax.experimental import pallas as pl
from jax.experimental.pallas import tpu as pltpu
from jax.sharding import PartitionSpec as P

MIXING_BLOCK = 128
BAND_BLOCKS = 16
NSTR = 2


EPS = 1e-05


def slot_mask(shape):
    slot_idx = lax.broadcasted_iota(jnp.int32, shape, 0)
    row_idx = lax.broadcasted_iota(jnp.int32, shape, 1)
    col_idx = lax.broadcasted_iota(jnp.int32, shape, 2)
    return (slot_idx > 0) | (row_idx >= col_idx)


def band_matrix(weights, backward):
    group = 2
    columns = group + BAND_BLOCKS - 1
    row_ids = jnp.arange(group, dtype=jnp.int32)[:, None]
    col_ids = jnp.arange(columns, dtype=jnp.int32)[None, :]
    if backward:
        offsets = col_ids - row_ids
    else:
        offsets = row_ids + BAND_BLOCKS - 1 - col_ids
    valid = (offsets >= 0) & (offsets < BAND_BLOCKS)
    clipped = jnp.clip(offsets, 0, BAND_BLOCKS - 1)
    tiles = jnp.take(weights[:BAND_BLOCKS], clipped.reshape(-1), axis=0)
    tiles = tiles.reshape(group, columns, MIXING_BLOCK, MIXING_BLOCK)
    if backward:
        tiles = jnp.swapaxes(tiles, 2, 3)
    tiles = jnp.where(valid[:, :, None, None], tiles, jnp.zeros((), tiles.dtype))
    return tiles.transpose(0, 2, 1, 3).reshape(group * MIXING_BLOCK, columns * MIXING_BLOCK)


def band_apply(matrix, padded, num_blocks, width):
    group = 2
    span_len = (group + BAND_BLOCKS - 1) * MIXING_BLOCK

    def one_group(group_id):
        piece = lax.dynamic_slice_in_dim(padded, group_id * group * MIXING_BLOCK, span_len, 0)
        return jnp.dot(matrix, piece, preferred_element_type=jnp.float32)

    result = lax.map(one_group, jnp.arange(num_blocks // group, dtype=jnp.int32))
    return result.reshape(num_blocks, MIXING_BLOCK, width)


def strided_blocks(blocks, stride_cols, strided):
    valid_rows = stride_cols[:, strided] >= 0
    safe_cols = jnp.maximum(stride_cols[:, strided], 0)
    picked = jnp.take(blocks, safe_cols, axis=0)
    return (
        jnp.where(valid_rows[:, None, None], picked, jnp.zeros((), picked.dtype)),
        valid_rows,
        safe_cols,
    )


def mix_forward(blocks, weights, stride_cols, mix_bias):
    num_blocks, _, width = blocks.shape
    tokens = blocks.reshape(num_blocks * MIXING_BLOCK, width)
    front = jnp.zeros(((BAND_BLOCKS - 1) * MIXING_BLOCK, width), blocks.dtype)
    padded = jnp.concatenate([front, tokens], axis=0)
    mixed_sum = band_apply(band_matrix(weights, False), padded, num_blocks, width)
    for strided in range(NSTR):
        picked, valid_rows, safe_cols = strided_blocks(blocks, stride_cols, strided)
        mixed_sum = mixed_sum + jnp.einsum(
            "ab,nbc->nac",
            weights[BAND_BLOCKS + strided],
            picked,
            preferred_element_type=jnp.float32,
        )
    mixed_sum = mixed_sum + mix_bias.reshape(num_blocks, MIXING_BLOCK, 1)
    return (mixed_sum.astype(jnp.bfloat16), padded)


def mix_backward(dblocks, blocks, padded, weights, stride_cols):
    num_blocks, _, width = blocks.shape
    total_len = num_blocks * MIXING_BLOCK
    dtokens = dblocks.reshape(total_len, width)
    tail = jnp.zeros(((BAND_BLOCKS - 1) * MIXING_BLOCK, width), dblocks.dtype)
    padded_back = jnp.concatenate([dtokens, tail], axis=0)
    dnorm = band_apply(band_matrix(weights, True), padded_back, num_blocks, width)
    band_grads = []
    for offset in range(BAND_BLOCKS):
        start = (BAND_BLOCKS - 1 - offset) * MIXING_BLOCK
        shifted = lax.slice_in_dim(padded, start, start + total_len, axis=0).reshape(
            num_blocks, MIXING_BLOCK, width
        )
        band_grads.append(
            jnp.einsum("nac,nbc->ab", dblocks, shifted, preferred_element_type=jnp.float32)
        )
    far_grads = []
    block_ids = jnp.arange(num_blocks, dtype=jnp.int32)
    for strided in range(NSTR):
        picked, valid_rows, safe_cols = strided_blocks(blocks, stride_cols, strided)
        far_grads.append(
            jnp.einsum("nac,nbc->ab", dblocks, picked, preferred_element_type=jnp.float32)
        )
        scatter_term = jnp.einsum(
            "ab,nac->nbc",
            weights[BAND_BLOCKS + strided],
            dblocks,
            preferred_element_type=jnp.float32,
        )
        scatter_term = jnp.where(
            valid_rows[:, None, None], scatter_term, jnp.zeros((), jnp.float32)
        )
        one_hot = (block_ids[:, None] == safe_cols[None, :]).astype(jnp.float32)
        dnorm = dnorm + jnp.einsum(
            "ji,ibc->jbc", one_hot, scatter_term, precision=lax.Precision.HIGHEST
        )
    slot_grad = jnp.stack(band_grads + far_grads)
    slot_grad = jnp.where(slot_mask(slot_grad.shape), slot_grad, jnp.zeros((), jnp.float32))
    return (dnorm.astype(jnp.bfloat16), slot_grad)


def shards(gated_part, mixed_part, out_grad, norm_gain, mix_bias, token_mixing_weight, stride_cols):
    seq_parts = lax.axis_size("seq")
    batch_size = lax.axis_size("dp")
    gated_rows = gated_part[0]
    value_rows = mixed_part[0]
    grad_rows = out_grad[0]
    tok_local, half_width = gated_rows.shape
    slice_width = half_width // seq_parts
    total_len = tok_local * seq_parts
    num_blocks = total_len // MIXING_BLOCK
    values = value_rows.astype(jnp.float32)
    row_mean = jnp.mean(values, axis=1, keepdims=True)
    centered = values - row_mean
    row_var = jnp.mean(centered * centered, axis=1, keepdims=True)
    inv_std = lax.rsqrt(row_var + EPS)
    norm_hat = centered * inv_std
    normed = (norm_hat * norm_gain).astype(jnp.bfloat16)
    weights = jnp.where(
        slot_mask(token_mixing_weight.shape),
        token_mixing_weight,
        jnp.zeros((), token_mixing_weight.dtype),
    )

    def to_panels(rows):
        return rows.reshape(tok_local, seq_parts, slice_width)

    def to_blocks(panel):
        return panel.reshape(num_blocks, MIXING_BLOCK, slice_width)

    def to_columns(blocks):
        return blocks.reshape(total_len, 1, slice_width)

    panel_norm = lax.all_to_all(to_panels(normed), "seq", split_axis=1, concat_axis=0, tiled=True)
    blocks = to_blocks(panel_norm)
    mixed16, padded = mix_forward(blocks, weights, stride_cols, mix_bias)
    mixed_rows = lax.all_to_all(
        to_columns(mixed16), "seq", split_axis=0, concat_axis=1, tiled=True
    ).reshape(tok_local, half_width)
    grad_f32 = grad_rows.astype(jnp.float32)
    gated_grad_rows = (grad_f32 * mixed_rows.astype(jnp.float32)).astype(jnp.bfloat16)
    dmix16 = (grad_f32 * gated_rows.astype(jnp.float32)).astype(jnp.bfloat16)
    local_bias = jnp.sum(dmix16.astype(jnp.float32), axis=1)
    bias_rows = lax.psum(local_bias, "dp")
    panel_dmix = lax.all_to_all(to_panels(dmix16), "seq", split_axis=1, concat_axis=0, tiled=True)
    dnorm16, slot_grad = mix_backward(to_blocks(panel_dmix), blocks, padded, weights, stride_cols)
    dnorm_rows = lax.all_to_all(
        to_columns(dnorm16), "seq", split_axis=0, concat_axis=1, tiled=True
    ).reshape(tok_local, half_width)
    dnorm_f32 = dnorm_rows.astype(jnp.float32)
    hat_grad = dnorm_f32 * norm_gain
    value_grad = inv_std * (
        hat_grad
        - jnp.mean(hat_grad, axis=1, keepdims=True)
        - norm_hat * jnp.mean(hat_grad * norm_hat, axis=1, keepdims=True)
    )
    gain_part = jnp.sum(dnorm_f32 * norm_hat, axis=0)
    slot_sum, gain_sum = lax.psum((slot_grad, gain_part), ("dp", "seq"))
    weight_grad = slot_sum / math.sqrt(batch_size * total_len * half_width)
    gain_grad = gain_sum / math.sqrt(batch_size * total_len)
    bias_grad = bias_rows / math.sqrt(batch_size * half_width)
    return (
        gated_grad_rows[None],
        value_grad.astype(jnp.bfloat16)[None],
        weight_grad,
        gain_grad,
        bias_grad,
    )


PAIR = 2 * MIXING_BLOCK
SEG = 256
BANDS = 12
Z_CHUNKS = (256, 512, 512)
O_CHUNKS = (256, 512)
ORDER = (("z", 0), ("o", 0), ("z", 1), ("o", 1), ("z", 2))
X_PAIRS = {"z": ((1, 0), (2, 3)), "o": ((0, 1), (3, 2))}
Y_PAIRS = {"z": ((2, 0), (1, 3)), "o": ((0, 2), (3, 1))}
D_PAIRS = {"z": ((0, 3), (3, 0)), "o": ((1, 2), (2, 1))}
SLOT_ROWS = 18 * 128
GAIN_ROWS = 32
BIAS_ROWS = 24
ACC_ROWS = SLOT_ROWS + GAIN_ROWS + BIAS_ROWS
F32 = jnp.float32
BF16 = jnp.bfloat16


def segment_starts():
    table = {}
    at = 0
    for width in (512, 256):
        for kind, chunks in (("z", Z_CHUNKS), ("o", O_CHUNKS)):
            for number, chunk in enumerate(chunks):
                if chunk == width:
                    table[kind, number] = (at, at + width, width)
                    at += 2 * width
    return table, at


def params(limit=56, **kw):
    return pltpu.CompilerParams(vmem_limit_bytes=limit * 1024 * 1024, **kw)


def nt_dot(left, right):
    return lax.dot_general(left, right, (((1,), (1,)), ((), ())), preferred_element_type=F32)


def dot(left, right):
    return jnp.dot(left, right, preferred_element_type=F32)


def prep_body(w_ref, v_ref, vt_ref, s_ref, st_ref):
    row = lax.broadcasted_iota(jnp.int32, (128, 128), 0)
    col = lax.broadcasted_iota(jnp.int32, (128, 128), 1)
    zero = jnp.zeros((128, 128), BF16)

    def block(slot):
        if slot < 0 or slot >= BAND_BLOCKS:
            return zero, zero
        value = w_ref[slot].astype(F32)
        if slot == 0:
            value = jnp.where(row >= col, value, 0.0)
        return value.astype(BF16), value.T.astype(BF16)

    for e in range(BANDS):
        for a in range(2):
            for b in range(2):
                value, turned = block(2 * e + a - b)
                v_ref[e, a * 128:(a + 1) * 128, b * 128:(b + 1) * 128] = value
                vt_ref[e, b * 128:(b + 1) * 128, a * 128:(a + 1) * 128] = turned
    for s in range(NSTR):
        value = w_ref[BAND_BLOCKS + s]
        s_ref[:, s * 128:(s + 1) * 128] = value
        st_ref[s * 128:(s + 1) * 128, :] = value.astype(F32).T.astype(BF16)


def prep(weights):
    return pl.pallas_call(
        prep_body,
        out_shape=(
            jax.ShapeDtypeStruct((BANDS, PAIR, PAIR), BF16),
            jax.ShapeDtypeStruct((BANDS, PAIR, PAIR), BF16),
            jax.ShapeDtypeStruct((128, PAIR), BF16),
            jax.ShapeDtypeStruct((PAIR, 128), BF16),
        ),
        compiler_params=params(),
        name="prep",
    )(weights)


def stats_body(v_ref, mean_ref, inv_ref):
    values = v_ref[...].astype(F32)
    mean = jnp.mean(values, axis=1, keepdims=True)
    centered = values - mean
    var = jnp.mean(centered * centered, axis=1, keepdims=True)
    mean_ref[...] = mean
    inv_ref[...] = lax.rsqrt(var + EPS)


def stats(value_rows):
    tokens, width = value_rows.shape
    col = pl.BlockSpec((128, 1), lambda i: (i, 0))
    return pl.pallas_call(
        stats_body,
        grid=(tokens // 128,),
        in_specs=[pl.BlockSpec((128, width), lambda i: (i, 0))],
        out_specs=[col, col],
        out_shape=[jax.ShapeDtypeStruct((tokens, 1), F32)] * 2,
        compiler_params=params(),
        name="stats",
    )(value_rows)


def pack_body(role, ma, mb, ga, gb, ua, ub, na, nb, mean_ref, inv_ref, xa, ya, xb, yb):
    last = role[0] == 3
    for m, g, u, n, x, y in ((ma, ga, ua, na, xa, ya), (mb, gb, ub, nb, xb, yb)):
        for i in range(6):
            rows = slice(i * 128, (i + 1) * 128)
            hat = (m[rows, :].astype(F32) - mean_ref[rows, :]) * inv_ref[rows, :]
            normed = hat * n[...]
            dmix = g[rows, :].astype(F32) * u[rows, :].astype(F32)
            x[i] = jnp.where(last, dmix, normed).astype(BF16)
            y[i] = jnp.where(last, normed, dmix).astype(BF16)


def pack(role, mixed, grad, gated, gain, mean, inv, first, second, width):
    tokens = mixed.shape[0]

    def spec_a(rows):
        return pl.BlockSpec((rows, SEG), lambda j, r: (0, jnp.where(r[0] < 2, first, second) // SEG + j))

    def spec_b(rows):
        return pl.BlockSpec((rows, SEG), lambda j, r: (0, jnp.where(r[0] < 2, second, first) // SEG + j))

    col = pl.BlockSpec((tokens, 1), lambda j, r: (0, 0))
    out = pl.BlockSpec((6, 128, SEG), lambda j, r: (0, 0, j))
    return pl.pallas_call(
        pack_body,
        grid_spec=pltpu.PrefetchScalarGridSpec(
            num_scalar_prefetch=1,
            grid=(width // SEG,),
            in_specs=[spec_a(tokens), spec_b(tokens)] * 3 + [spec_a(1), spec_b(1), col, col],
            out_specs=[out] * 4,
        ),
        out_shape=[jax.ShapeDtypeStruct((6, 128, width), BF16)] * 4,
        compiler_params=params(),
        name="pack",
    )(role, mixed, mixed, grad, grad, gated, gated, gain, gain, mean, inv)


def fold_slots(vg_ref, acc_ref, bands, add):
    for e in bands:
        for a in range(2):
            for b in range(2):
                slot = 2 * e + a - b
                if slot < 0 or slot >= BAND_BLOCKS or a == 1 and b == 1:
                    continue
                value = vg_ref[e, a * 128:(a + 1) * 128, b * 128:(b + 1) * 128]
                if a == b:
                    value = value + vg_ref[e, 128:, 128:]
                rows = slice(slot * 128, (slot + 1) * 128)
                acc_ref[rows, :] = acc_ref[rows, :] + value


def local_body(role, m, g, u, n, mean_ref, inv_ref, v_ref, vt_ref, mo, no, acc, vg, a_s, d_s, bias):
    step = pl.program_id(0)

    @pl.when(step == 0)
    def _():
        vg[...] = jnp.zeros_like(vg)
        bias[...] = jnp.zeros_like(bias)
        acc[...] = jnp.zeros_like(acc)

    width = m.shape[1]
    for p in range(3):
        rows = slice(p * PAIR, (p + 1) * PAIR)
        hat = (m[rows, :].astype(F32) - mean_ref[rows, :]) * inv_ref[rows, :]
        a_s[p] = (hat * n[...]).astype(BF16)
        d_s[p] = (g[rows, :].astype(F32) * u[rows, :].astype(F32)).astype(BF16)
    ones = jnp.ones((8, width), BF16)
    gain = jnp.zeros((1, width), F32)
    for p in range(3):
        mixed = dot(v_ref[0], a_s[p])
        dnorm = dot(vt_ref[0], d_s[p])
        vg[0] = vg[0] + nt_dot(d_s[p], a_s[p])
        for e in range(1, 3):
            if p - e >= 0:
                mixed = mixed + dot(v_ref[e], a_s[p - e])
                vg[e] = vg[e] + nt_dot(d_s[p], a_s[p - e])
            if p + e < 3:
                dnorm = dnorm + dot(vt_ref[e], d_s[p + e])
        rows = slice(p * PAIR, (p + 1) * PAIR)
        mo[rows, :] = mixed.astype(BF16)
        no[rows, :] = dnorm.astype(BF16)
        gain = gain + jnp.sum(dnorm * a_s[p].astype(F32), axis=0, keepdims=True)
        bias[:, rows] = bias[:, rows] + nt_dot(ones, d_s[p])
    gain = gain / n[...]
    for k in range(width // 128):
        acc[pl.ds(SLOT_ROWS + step * (width // 128) + k, 1), :] = gain[:, k * 128:(k + 1) * 128]

    @pl.when(step == pl.num_programs(0) - 1)
    def _():
        fold_slots(vg, acc, range(3), True)
        row = lax.broadcasted_iota(jnp.int32, (128, 128), 0)
        col = lax.broadcasted_iota(jnp.int32, (128, 128), 1)
        acc[:128, :] = jnp.where(row >= col, acc[:128, :], 0.0)
        for k in range(6):
            acc[pl.ds(SLOT_ROWS + GAIN_ROWS + role[0] * 6 + k, 1), :] = bias[0:1, k * 128:(k + 1) * 128]


def local_part(role, mixed, grad, gated, gain, mean, inv, v, vt):
    tokens, full = mixed.shape
    width = 512
    block = pl.BlockSpec((tokens, width), lambda j, r: (0, j))
    col = pl.BlockSpec((tokens, 1), lambda j, r: (0, 0))
    band = pl.BlockSpec((3, PAIR, PAIR), lambda j, r: (0, 0, 0))
    return pl.pallas_call(
        local_body,
        grid_spec=pltpu.PrefetchScalarGridSpec(
            num_scalar_prefetch=1,
            grid=(full // width,),
            in_specs=[block, block, block, pl.BlockSpec((1, width), lambda j, r: (0, j)), col, col, band, band],
            out_specs=[block, block, pl.BlockSpec((ACC_ROWS, 128), lambda j, r: (0, 0))],
            scratch_shapes=[
                pltpu.VMEM((3, PAIR, PAIR), F32),
                pltpu.VMEM((3, PAIR, width), BF16),
                pltpu.VMEM((3, PAIR, width), BF16),
                pltpu.VMEM((8, tokens), F32),
            ],
        ),
        out_shape=[
            jax.ShapeDtypeStruct((tokens, full), BF16),
            jax.ShapeDtypeStruct((tokens, full), BF16),
            jax.ShapeDtypeStruct((ACC_ROWS, 128), F32),
        ],
        compiler_params=params(),
        name="local_part",
    )(role, mixed, grad, gated, gain, mean, inv, v, vt)


def owner_body(kind, width, first, second):
    mine = (0, 3) if kind == "z" else (1, 2)
    starts = {mine[0]: first, mine[1]: second}

    def body(role, cols, xa, ya, r0, r1, r2, r3, r4, gain_ref, v_ref, vt_ref, s_ref, st_ref, acc_in,
             o0, o1, o2, o3, o4, o5, acc_out,
             a_s, d_s, m_f, n_f, m_s, n_s, vg, sg, acc_s, in_sem, acc_sem, m_sem, n_sem):
        r = role[0]

        def third(buf, k):
            return buf.at[pl.ds(6 * k, 6)]

        if kind == "z":
            sources = {0: (xa, r0, r2, r1, r3, r4), 3: (r4, r2, r0, r3, r1, xa)}
            targets = {0: ((o0, o2, o4), (o5, o1, o3)), 3: ((o2, o0, o5), (o4, o3, o1))}
        else:
            sources = {1: (r0, xa, r2, ya, r3, r1), 2: (r1, r2, xa, r3, ya, r0)}
            targets = {1: ((o0, o4, o3), (o2, o1, o5)), 2: ((o4, o0, o2), (o3, o5, o1))}
        places = [third(a_s, 0), third(a_s, 1), third(a_s, 2), third(d_s, 0), third(d_s, 1), third(d_s, 2)]

        @pl.when((r == mine[0]) | (r == mine[1]))
        def _():
            fetch = pltpu.make_async_copy(acc_in, acc_s, acc_sem)
            fetch.start()
            for who in mine:
                @pl.when(r == who)
                def _():
                    copies = [
                        pltpu.make_async_copy(src, dst, in_sem.at[k])
                        for k, (src, dst) in enumerate(zip(sources[who], places))
                    ]
                    for copy in copies:
                        copy.start()
            vg[...] = jnp.zeros_like(vg)
            sg[...] = jnp.zeros_like(sg)
            m_f[...] = jnp.zeros_like(m_f)
            n_f[...] = jnp.zeros_like(n_f)
            for k in range(6):
                pltpu.make_async_copy(xa, places[k], in_sem.at[k]).wait()

            def pair(buf, p, at):
                return buf[pl.ds(2 * p, 2), :, at:at + SEG].reshape(PAIR, SEG)

            for at in range(0, width, SEG):
                def strided(i, carry):
                    c0 = cols[BAND_BLOCKS + i, 0]
                    c1 = cols[BAND_BLOCKS + i, 1]
                    picked = jnp.concatenate([a_s[c0, :, at:at + SEG], a_s[c1, :, at:at + SEG]], axis=0)
                    dmix = d_s[10 + i, :, at:at + SEG]
                    m_f[10 + i, :, at:at + SEG] = dot(s_ref[...], picked)
                    back = dot(st_ref[...], dmix)
                    n_f[c0, :, at:at + SEG] = n_f[c0, :, at:at + SEG] + back[:128]
                    n_f[c1, :, at:at + SEG] = n_f[c1, :, at:at + SEG] + back[128:]
                    sg[...] = sg[...] + nt_dot(dmix, picked)
                    return carry

                lax.fori_loop(0, 8, strided, 0)

                for dev in range(1, 4):
                    lows = range(1 if dev == 3 else 0, 3 * dev)

                    def forward(t, carry):
                        dmix = pair(d_s, 3 * (dev - 1) + t, at)
                        total = pair(m_f, 3 * (dev - 1) + t, at)
                        for p in lows:
                            total = total + dot(v_ref[3 * dev + t - p], pair(a_s, p, at))
                        m_s[pl.ds(6 * (dev - 1) + 2 * t, 2), :, at:at + SEG] = total.astype(BF16).reshape(2, 128, SEG)
                        for p in lows:
                            e = 3 * dev + t - p
                            vg[e] = vg[e] + nt_dot(dmix, pair(a_s, p, at))
                        return carry

                    lax.fori_loop(0, 3, forward, 0)

            for who in mine:
                @pl.when(r == who)
                def _():
                    for k in range(3):
                        pltpu.make_async_copy(third(m_s, k), targets[who][0][k], m_sem.at[k]).start()

            for at in range(0, width, SEG):
                total_gain = jnp.zeros((1, SEG), F32)
                for dev in range(3):
                    highs = range(3 * dev + 3, 11 if dev == 0 else 12)

                    def backward(t, gain):
                        total = pair(n_f, 3 * dev + t, at)
                        for g in highs:
                            total = total + dot(vt_ref[g - 3 * dev - t], pair(d_s, g - 3, at))
                        n_s[pl.ds(6 * dev + 2 * t, 2), :, at:at + SEG] = total.astype(BF16).reshape(2, 128, SEG)
                        normed = pair(a_s, 3 * dev + t, at).astype(F32)
                        return gain + jnp.sum(total * normed, axis=0, keepdims=True)

                    total_gain = lax.fori_loop(0, 3, backward, total_gain)
                m_gain = total_gain / gain_ref[:, at:at + SEG]
                sg_row = m_gain
                if at == 0:
                    fetch.wait()
                base = jnp.where(r == mine[0], first, second) // 128
                for k in range(SEG // 128):
                    where = pl.ds(SLOT_ROWS + base + at // 128 + k, 1)
                    acc_s[where, :] = acc_s[where, :] + sg_row[:, k * 128:(k + 1) * 128]

            for who in mine:
                @pl.when(r == who)
                def _():
                    for k in range(3):
                        pltpu.make_async_copy(third(n_s, k), targets[who][1][k], n_sem.at[k]).start()

            fold_slots(vg, acc_s, range(1, 9), True)
            for s in range(NSTR):
                rows = slice((BAND_BLOCKS + s) * 128, (BAND_BLOCKS + s + 1) * 128)
                acc_s[rows, :] = acc_s[rows, :] + sg[:, s * 128:(s + 1) * 128]
            put = pltpu.make_async_copy(acc_s, acc_out, acc_sem)
            put.start()
            for k in range(3):
                pltpu.make_async_copy(third(m_s, k), o0, m_sem.at[k]).wait()
                pltpu.make_async_copy(third(n_s, k), o0, n_sem.at[k]).wait()
            put.wait()

    return body


def owner(kind, first, second, width, role, cols, xa, ya, received, gain, tables, acc):
    received = list(received)
    while len(received) < 5:
        received.append(received[-1])
    hbm = pl.BlockSpec(memory_space=pl.ANY)
    v, vt, s, st = tables
    mine = (0, 3) if kind == "z" else (1, 2)

    def gain_at(i, r, c):
        return (0, jnp.where(r[0] == mine[1], second, first) // width)

    def whole(shape):
        return pl.BlockSpec(shape, lambda i, r, c: (0,) * len(shape))

    piece = jax.ShapeDtypeStruct((6, 128, width), BF16)
    return pl.pallas_call(
        owner_body(kind, width, first, second),
        grid_spec=pltpu.PrefetchScalarGridSpec(
            num_scalar_prefetch=2,
            grid=(1,),
            in_specs=[hbm] * 7
            + [pl.BlockSpec((1, width), gain_at), whole(v.shape), whole(vt.shape), whole(s.shape), whole(st.shape), hbm],
            out_specs=[hbm] * 7,
            scratch_shapes=[
                pltpu.VMEM((18, 128, width), BF16),
                pltpu.VMEM((18, 128, width), BF16),
                pltpu.VMEM((18, 128, width), F32),
                pltpu.VMEM((18, 128, width), F32),
                pltpu.VMEM((18, 128, width), BF16),
                pltpu.VMEM((18, 128, width), BF16),
                pltpu.VMEM((BANDS, PAIR, PAIR), F32),
                pltpu.VMEM((128, PAIR), F32),
                pltpu.VMEM((ACC_ROWS, 128), F32),
                pltpu.SemaphoreType.DMA((6,)),
                pltpu.SemaphoreType.DMA,
                pltpu.SemaphoreType.DMA((3,)),
                pltpu.SemaphoreType.DMA((3,)),
            ],
        ),
        out_shape=[piece] * 6 + [jax.ShapeDtypeStruct((ACC_ROWS, 128), F32)],
        input_output_aliases={14: 6},
        compiler_params=params(),
        name="owner_" + kind,
    )(role, cols, xa, ya, *received, gain, v, vt, s, st, acc)


def finish_body(table, rows, full):
    def body(role, m, g, ml, nl, n, mean_ref, inv_ref, bias_ref, *rest):
        pieces = rest[: 6 * len(table)]
        gated_out, value_out, hat_s, grad_s = rest[6 * len(table):]
        r = role[0]
        mean = mean_ref[...]
        inv = inv_ref[...]
        bias = bias_ref[...]
        edge = (r == 0) | (r == 3)
        sum_one = jnp.zeros((rows, 128), F32)
        sum_two = jnp.zeros((rows, 128), F32)
        for index, (first, second, width) in enumerate(table):
            for side in range(2):
                low = jnp.where(r < 2, first, second) if side == 0 else jnp.where(r < 2, second, first)
                single, both_m, both_n = pieces[6 * index + 3 * side: 6 * index + 3 * side + 3]
                for at in range(0, width, SEG):
                    here = pl.ds(pl.multiple_of(low + at, SEG), SEG)
                    there = slice(at, at + SEG)
                    one = single[0, :, there].astype(F32)
                    off_m = jnp.where(edge, jnp.where(r == 3, one, 0.0), both_m[0, :, there].astype(F32))
                    off_n = jnp.where(edge, jnp.where(r == 0, one, 0.0), both_n[0, :, there].astype(F32))
                    mixed = (off_m + ml[:, here].astype(F32) + bias).astype(BF16).astype(F32)
                    gated_out[:, here] = (g[:, here].astype(F32) * mixed).astype(BF16)
                    dnorm = (off_n + nl[:, here].astype(F32)).astype(BF16).astype(F32)
                    hat = (m[:, here].astype(F32) - mean) * inv
                    grad = dnorm * n[:, here]
                    hat_s[:, here] = hat
                    grad_s[:, here] = grad
                    prod = grad * hat
                    for k in range(SEG // 128):
                        sum_one = sum_one + grad[:, k * 128:(k + 1) * 128]
                        sum_two = sum_two + prod[:, k * 128:(k + 1) * 128]
        mean_one = jnp.sum(sum_one, axis=1, keepdims=True) * (1.0 / full)
        mean_two = jnp.sum(sum_two, axis=1, keepdims=True) * (1.0 / full)
        for at in range(0, full, 512):
            here = slice(at, at + 512)
            value = inv * (grad_s[:, here] - mean_one - hat_s[:, here] * mean_two)
            value_out[:, here] = value.astype(BF16)

    return body


def finish(role, mixed, grad, m_loc, n_loc, gain, mean, inv, bias, table, pieces):
    tokens, full = mixed.shape
    rows = 64
    row = pl.BlockSpec((rows, full), lambda i, r: (i, 0))
    col = pl.BlockSpec((rows, 1), lambda i, r: (i, 0))

    def piece(width):
        return pl.BlockSpec((1, rows, width), lambda i, r: (i // (128 // rows), i % (128 // rows), 0))

    return pl.pallas_call(
        finish_body(table, rows, full),
        grid_spec=pltpu.PrefetchScalarGridSpec(
            num_scalar_prefetch=1,
            grid=(tokens // rows,),
            in_specs=[row] * 4
            + [pl.BlockSpec((1, full), lambda i, r: (0, 0)), col, col, col]
            + [piece(p.shape[-1]) for p in pieces],
            out_specs=[row, row],
            scratch_shapes=[pltpu.VMEM((rows, full), F32), pltpu.VMEM((rows, full), F32)],
        ),
        out_shape=[jax.ShapeDtypeStruct((tokens, full), BF16)] * 2,
        compiler_params=params(),
        name="finish",
    )(role, mixed, grad, m_loc, n_loc, gain, mean, inv, bias, *pieces)


def move(value, pairs):
    return lax.ppermute(value, "seq", pairs)


def shards_of_four(gated_part, mixed_part, out_grad, norm_gain, mix_bias, token_mixing_weight, stride_cols):
    batch_size = lax.axis_size("dp")
    seq_parts = lax.axis_size("seq")
    gated, mixed, grad = gated_part[0], mixed_part[0], out_grad[0]
    tokens, full = mixed.shape
    index = lax.axis_index("seq").astype(jnp.int32)
    role = index.reshape(1)
    gain = norm_gain.reshape(1, full)
    starts, _ = segment_starts()
    mean, inv = stats(mixed)
    sent = {}
    for key in ORDER:
        sent[key] = pack(role, mixed, grad, gated, gain, mean, inv, *starts[key])
    tables = prep(token_mixing_weight)
    received = {}
    for key in ORDER:
        kind = key[0]
        xa, ya, xb, yb = sent[key]
        xs, ys, ds = X_PAIRS[kind], Y_PAIRS[kind], D_PAIRS[kind]
        if kind == "z":
            received[key] = (move(xa, xs), move(ya, xs), move(xb, ys), move(yb, ys), move(xb, ds))
        else:
            received[key] = (move(xa, xs), move(xb, ys), move(xb, ds), move(yb, ds))
    m_loc, n_loc, acc = local_part(role, mixed, grad, gated, gain, mean, inv, tables[0], tables[1])
    pieces = []
    table = []
    for key in ORDER:
        kind = key[0]
        first, second, width = starts[key]
        xa, ya, _, _ = sent[key]
        *out, acc = owner(kind, first, second, width, role, stride_cols, xa, ya, received[key], gain, tables, acc)
        if kind == "z":
            xs, ys, ds = ((0, 1), (3, 2)), ((0, 2), (3, 1)), ((0, 3), (3, 0))
            far = move(out[4], ds)
            pieces += [out[5], move(out[0], xs), move(out[1], xs), far, move(out[2], ys), move(out[3], ys)]
        else:
            xs, ys, ds = ((1, 0), (2, 3)), ((1, 3), (2, 0)), ((1, 2), (2, 1))
            pieces += [move(out[2], xs), out[0], out[1], move(out[3], ys), move(out[4], ds), move(out[5], ds)]
        table.append((first, second, width))
    total = lax.psum(acc, ("dp", "seq"))
    bias_col = lax.dynamic_slice_in_dim(mix_bias, index * tokens, tokens, 0).reshape(tokens, 1)
    gated_grad, value_grad = finish(role, mixed, grad, m_loc, n_loc, gain, mean, inv, bias_col, table, pieces)
    total_len = tokens * seq_parts
    weight_grad = total[:SLOT_ROWS].reshape(18, 128, 128) / math.sqrt(batch_size * total_len * full)
    gain_grad = total[SLOT_ROWS:SLOT_ROWS + GAIN_ROWS].reshape(full) / math.sqrt(batch_size * total_len)
    bias_rows = lax.dynamic_slice_in_dim(total, SLOT_ROWS + GAIN_ROWS + index * 6, 6, 0).reshape(tokens)
    bias_grad = bias_rows / math.sqrt(batch_size * full)
    return (gated_grad[None], value_grad[None], weight_grad, gain_grad, bias_grad)


def solution(mesh):
    placed = (P("dp", "seq", None), P("dp", "seq", None), P("dp", "seq", None), P(), P(), P(), P())
    return jax.shard_map(
        shards_of_four if mesh.shape["seq"] == 4 else shards,
        mesh=mesh,
        in_specs=placed,
        out_specs=(P("dp", "seq", None), P("dp", "seq", None), P(), P(), P("seq")),
        check_vma=False,
    )
```

```python
import math

import jax
import jax.numpy as jnp
from jax import lax
from jax.experimental import pallas as pl
from jax.experimental.pallas import tpu as pltpu
from jax.sharding import PartitionSpec as P


MIXING_BLOCK = 128
BAND_BLOCKS = 16
NSTR = 2


EPS = 1e-05


def slot_mask(shape):
    slot_idx = lax.broadcasted_iota(jnp.int32, shape, 0)
    row_idx = lax.broadcasted_iota(jnp.int32, shape, 1)
    col_idx = lax.broadcasted_iota(jnp.int32, shape, 2)
    return (slot_idx > 0) | (row_idx >= col_idx)


def band_matrix(weights, backward):
    group = 2
    columns = group + BAND_BLOCKS - 1
    row_ids = jnp.arange(group, dtype=jnp.int32)[:, None]
    col_ids = jnp.arange(columns, dtype=jnp.int32)[None, :]
    if backward:
        offsets = col_ids - row_ids
    else:
        offsets = row_ids + BAND_BLOCKS - 1 - col_ids
    valid = (offsets >= 0) & (offsets < BAND_BLOCKS)
    clipped = jnp.clip(offsets, 0, BAND_BLOCKS - 1)
    tiles = jnp.take(weights[:BAND_BLOCKS], clipped.reshape(-1), axis=0)
    tiles = tiles.reshape(group, columns, MIXING_BLOCK, MIXING_BLOCK)
    if backward:
        tiles = jnp.swapaxes(tiles, 2, 3)
    tiles = jnp.where(valid[:, :, None, None], tiles, jnp.zeros((), tiles.dtype))
    return tiles.transpose(0, 2, 1, 3).reshape(group * MIXING_BLOCK, columns * MIXING_BLOCK)


def band_apply(matrix, padded, num_blocks, width):
    group = 2
    span_len = (group + BAND_BLOCKS - 1) * MIXING_BLOCK

    def one_group(group_id):
        piece = lax.dynamic_slice_in_dim(padded, group_id * group * MIXING_BLOCK, span_len, 0)
        return jnp.dot(matrix, piece, preferred_element_type=jnp.float32)

    result = lax.map(one_group, jnp.arange(num_blocks // group, dtype=jnp.int32))
    return result.reshape(num_blocks, MIXING_BLOCK, width)


def strided_blocks(blocks, stride_cols, strided):
    valid_rows = stride_cols[:, strided] >= 0
    safe_cols = jnp.maximum(stride_cols[:, strided], 0)
    picked = jnp.take(blocks, safe_cols, axis=0)
    return (
        jnp.where(valid_rows[:, None, None], picked, jnp.zeros((), picked.dtype)),
        valid_rows,
        safe_cols,
    )


def mix_forward(blocks, weights, stride_cols, mix_bias):
    num_blocks, _, width = blocks.shape
    tokens = blocks.reshape(num_blocks * MIXING_BLOCK, width)
    front = jnp.zeros(((BAND_BLOCKS - 1) * MIXING_BLOCK, width), blocks.dtype)
    padded = jnp.concatenate([front, tokens], axis=0)
    mixed_sum = band_apply(band_matrix(weights, False), padded, num_blocks, width)
    for strided in range(NSTR):
        picked, _, _ = strided_blocks(blocks, stride_cols, strided)
        mixed_sum = mixed_sum + jnp.einsum(
            "ab,nbc->nac",
            weights[BAND_BLOCKS + strided],
            picked,
            preferred_element_type=jnp.float32,
        )
    mixed_sum = mixed_sum + mix_bias.reshape(num_blocks, MIXING_BLOCK, 1)
    return (mixed_sum.astype(jnp.bfloat16), padded)


def mix_backward(dblocks, blocks, padded, weights, stride_cols):
    num_blocks, _, width = blocks.shape
    total_len = num_blocks * MIXING_BLOCK
    dtokens = dblocks.reshape(total_len, width)
    tail = jnp.zeros(((BAND_BLOCKS - 1) * MIXING_BLOCK, width), dblocks.dtype)
    padded_back = jnp.concatenate([dtokens, tail], axis=0)
    dnorm = band_apply(band_matrix(weights, True), padded_back, num_blocks, width)
    band_grads = []
    for offset in range(BAND_BLOCKS):
        start = (BAND_BLOCKS - 1 - offset) * MIXING_BLOCK
        shifted = lax.slice_in_dim(padded, start, start + total_len, axis=0).reshape(
            num_blocks, MIXING_BLOCK, width
        )
        band_grads.append(
            jnp.einsum("nac,nbc->ab", dblocks, shifted, preferred_element_type=jnp.float32)
        )
    far_grads = []
    block_ids = jnp.arange(num_blocks, dtype=jnp.int32)
    for strided in range(NSTR):
        picked, valid_rows, safe_cols = strided_blocks(blocks, stride_cols, strided)
        far_grads.append(
            jnp.einsum("nac,nbc->ab", dblocks, picked, preferred_element_type=jnp.float32)
        )
        scatter_term = jnp.einsum(
            "ab,nac->nbc",
            weights[BAND_BLOCKS + strided],
            dblocks,
            preferred_element_type=jnp.float32,
        )
        scatter_term = jnp.where(
            valid_rows[:, None, None], scatter_term, jnp.zeros((), jnp.float32)
        )
        one_hot = (block_ids[:, None] == safe_cols[None, :]).astype(jnp.float32)
        dnorm = dnorm + jnp.einsum(
            "ji,ibc->jbc", one_hot, scatter_term, precision=lax.Precision.HIGHEST
        )
    slot_grad = jnp.stack(band_grads + far_grads)
    slot_grad = jnp.where(slot_mask(slot_grad.shape), slot_grad, jnp.zeros((), jnp.float32))
    return (dnorm.astype(jnp.bfloat16), slot_grad)


def shards(gated_part, mixed_part, out_grad, norm_gain, mix_bias, token_mixing_weight, stride_cols):
    seq_parts = lax.axis_size("seq")
    batch_size = lax.axis_size("dp")
    gated_rows = gated_part[0]
    value_rows = mixed_part[0]
    grad_rows = out_grad[0]
    tok_local, half_width = gated_rows.shape
    slice_width = half_width // seq_parts
    total_len = tok_local * seq_parts
    num_blocks = total_len // MIXING_BLOCK
    values = value_rows.astype(jnp.float32)
    row_mean = jnp.mean(values, axis=1, keepdims=True)
    centered = values - row_mean
    row_var = jnp.mean(centered * centered, axis=1, keepdims=True)
    inv_std = lax.rsqrt(row_var + EPS)
    norm_hat = centered * inv_std
    normed = (norm_hat * norm_gain).astype(jnp.bfloat16)
    weights = jnp.where(
        slot_mask(token_mixing_weight.shape),
        token_mixing_weight,
        jnp.zeros((), token_mixing_weight.dtype),
    )

    def to_panels(rows):
        return rows.reshape(tok_local, seq_parts, slice_width)

    def to_blocks(panel):
        return panel.reshape(num_blocks, MIXING_BLOCK, slice_width)

    def to_columns(blocks):
        return blocks.reshape(total_len, 1, slice_width)

    panel_norm = lax.all_to_all(to_panels(normed), "seq", split_axis=1, concat_axis=0, tiled=True)
    blocks = to_blocks(panel_norm)
    mixed16, padded = mix_forward(blocks, weights, stride_cols, mix_bias)
    mixed_rows = lax.all_to_all(
        to_columns(mixed16), "seq", split_axis=0, concat_axis=1, tiled=True
    ).reshape(tok_local, half_width)
    grad_f32 = grad_rows.astype(jnp.float32)
    gated_grad_rows = (grad_f32 * mixed_rows.astype(jnp.float32)).astype(jnp.bfloat16)
    dmix16 = (grad_f32 * gated_rows.astype(jnp.float32)).astype(jnp.bfloat16)
    local_bias = jnp.sum(dmix16.astype(jnp.float32), axis=1)
    bias_rows = lax.psum(local_bias, "dp")
    panel_dmix = lax.all_to_all(to_panels(dmix16), "seq", split_axis=1, concat_axis=0, tiled=True)
    dnorm16, slot_grad = mix_backward(to_blocks(panel_dmix), blocks, padded, weights, stride_cols)
    dnorm_rows = lax.all_to_all(
        to_columns(dnorm16), "seq", split_axis=0, concat_axis=1, tiled=True
    ).reshape(tok_local, half_width)
    dnorm_f32 = dnorm_rows.astype(jnp.float32)
    hat_grad = dnorm_f32 * norm_gain
    value_grad = inv_std * (
        hat_grad
        - jnp.mean(hat_grad, axis=1, keepdims=True)
        - norm_hat * jnp.mean(hat_grad * norm_hat, axis=1, keepdims=True)
    )
    gain_part = jnp.sum(dnorm_f32 * norm_hat, axis=0)
    slot_sum, gain_sum = lax.psum((slot_grad, gain_part), ("dp", "seq"))
    weight_grad = slot_sum / math.sqrt(batch_size * total_len * half_width)
    gain_grad = gain_sum / math.sqrt(batch_size * total_len)
    bias_grad = bias_rows / math.sqrt(batch_size * half_width)
    return (
        gated_grad_rows[None],
        value_grad.astype(jnp.bfloat16)[None],
        weight_grad,
        gain_grad,
        bias_grad,
    )


PAIR = 2 * MIXING_BLOCK
SEG = 256
BANDS = 12
Z_CHUNKS = (512, 512, 256)
O_CHUNKS = (768,)
ORDER = (("z", 0), ("o", 0), ("z", 1), ("z", 2))
X_PAIRS = {"z": ((1, 0), (2, 3)), "o": ((0, 1), (3, 2))}
Y_PAIRS = {"z": ((2, 0), (1, 3)), "o": ((0, 2), (3, 1))}
D_PAIRS = {"z": ((0, 3), (3, 0)), "o": ((1, 2), (2, 1))}
SLOT_ROWS = 18 * 128
GAIN_ROWS = 32
ACC_ROWS = 2560
F32 = jnp.float32
BF16 = jnp.bfloat16


def segment_starts():
    table = {}
    at = 0
    for width in sorted(set(Z_CHUNKS + O_CHUNKS), reverse=True):
        for kind, chunks in (("z", Z_CHUNKS), ("o", O_CHUNKS)):
            for number, chunk in enumerate(chunks):
                if chunk == width:
                    table[kind, number] = (at, at + width, width)
                    at += 2 * width
    return table


def params(limit=56, **kw):
    return pltpu.CompilerParams(vmem_limit_bytes=limit * 1024 * 1024, **kw)


def nt_dot(left, right):
    return lax.dot_general(left, right, (((1,), (1,)), ((), ())), preferred_element_type=F32)


def dot(left, right):
    return jnp.dot(left, right, preferred_element_type=F32)


def prep_body(w_ref, v_ref, vt_ref, s_ref, st_ref):
    row = lax.broadcasted_iota(jnp.int32, (128, 128), 0)
    col = lax.broadcasted_iota(jnp.int32, (128, 128), 1)
    zero = jnp.zeros((128, 128), BF16)

    def block(slot):
        if slot < 0 or slot >= BAND_BLOCKS:
            return zero, zero
        value = w_ref[slot].astype(F32)
        if slot == 0:
            value = jnp.where(row >= col, value, 0.0)
        return value.astype(BF16), value.T.astype(BF16)

    for e in range(BANDS):
        for a in range(2):
            for b in range(2):
                value, turned = block(2 * e + a - b)
                down = (BANDS - 1 - e) * PAIR
                v_ref[a * 128:(a + 1) * 128, down + b * 128:down + (b + 1) * 128] = value
                vt_ref[b * 128:(b + 1) * 128, e * PAIR + a * 128:e * PAIR + (a + 1) * 128] = turned
    for s in range(NSTR):
        value = w_ref[BAND_BLOCKS + s]
        s_ref[:, s * 128:(s + 1) * 128] = value
        st_ref[s * 128:(s + 1) * 128, :] = value.astype(F32).T.astype(BF16)


def prep(weights):
    return pl.pallas_call(
        prep_body,
        out_shape=(
            jax.ShapeDtypeStruct((PAIR, BANDS * PAIR), BF16),
            jax.ShapeDtypeStruct((PAIR, BANDS * PAIR), BF16),
            jax.ShapeDtypeStruct((128, PAIR), BF16),
            jax.ShapeDtypeStruct((PAIR, 128), BF16),
        ),
        compiler_params=params(),
        name="prep",
    )(weights)


def stats_body(v_ref, mean_ref, inv_ref):
    values = v_ref[...].astype(F32)
    mean = jnp.mean(values, axis=1, keepdims=True)
    centered = values - mean
    var = jnp.mean(centered * centered, axis=1, keepdims=True)
    mean_ref[...] = jnp.broadcast_to(mean, mean_ref.shape)
    inv_ref[...] = jnp.broadcast_to(lax.rsqrt(var + EPS), inv_ref.shape)


def stats(value_rows):
    tokens, width = value_rows.shape
    rows = 192
    col = pl.BlockSpec((rows, 128), lambda i: (i, 0))
    return pl.pallas_call(
        stats_body,
        grid=(tokens // rows,),
        in_specs=[pl.BlockSpec((rows, width), lambda i: (i, 0))],
        out_specs=[col, col],
        out_shape=[jax.ShapeDtypeStruct((tokens, 128), F32)] * 2,
        compiler_params=params(),
        name="stats",
    )(value_rows)


def hat_of(m, mean, inv):
    parts = [(m[:, k:k + 128].astype(F32) - mean) * inv for k in range(0, m.shape[1], 128)]
    return jnp.concatenate(parts, axis=1)


def pack_body(kind):
    def body(role, ma, mb, ga, gb, ua, ub, na, nb, mean_ref, inv_ref, a_out, b_out, c_out, *more):
        last = role[0] == 3
        for side, (m, g, u, n) in enumerate(((ma, ga, ua, na), (mb, gb, ub, nb))):
            for i in range(3):
                rows = slice(i * 128, (i + 1) * 128)
                at = pl.ds(pl.multiple_of(pl.program_id(1) * 384 + i * 128, 128), 128)
                hat = hat_of(m[rows, :], mean_ref[at, :], inv_ref[at, :])
                normed = hat * n[...]
                dmix = g[rows, :].astype(F32) * u[rows, :].astype(F32)
                x = jnp.where(last, dmix, normed).astype(BF16)
                y = jnp.where(last, normed, dmix).astype(BF16)
                out = b_out if side else a_out
                out[0, i] = x
                out[1, i] = y
                if side == 1:
                    c_out[i] = x
                elif kind == "o":
                    more[0][i] = x

    return body


def pack(kind, role, mixed, grad, gated, gain, mean, inv, first, second, width):
    tokens = mixed.shape[0]

    def left(r):
        return jnp.where(r[0] < 2, first, second) // SEG

    def right(r):
        return jnp.where(r[0] < 2, second, first) // SEG

    main = [pl.BlockSpec((384, SEG), lambda j, i, r: (i, left(r) + j)), pl.BlockSpec((384, SEG), lambda j, i, r: (i, right(r) + j))]
    line = [pl.BlockSpec((1, SEG), lambda j, i, r: (0, left(r) + j)), pl.BlockSpec((1, SEG), lambda j, i, r: (0, right(r) + j))]
    col = pl.BlockSpec((tokens, 128), lambda j, i, r: (0, 0))
    two = pl.BlockSpec((2, 3, 128, SEG), lambda j, i, r: (0, i, 0, j))
    one = pl.BlockSpec((3, 128, SEG), lambda j, i, r: (i, 0, j))
    count = 2 if kind == "o" else 1
    return pl.pallas_call(
        pack_body(kind),
        grid_spec=pltpu.PrefetchScalarGridSpec(
            num_scalar_prefetch=1,
            grid=(width // SEG, tokens // 384),
            in_specs=main * 3 + line + [col, col],
            out_specs=[two, two] + [one] * count,
        ),
        out_shape=[jax.ShapeDtypeStruct((2, 6, 128, width), BF16)] * 2
        + [jax.ShapeDtypeStruct((6, 128, width), BF16)] * count,
        compiler_params=params(),
        name="pack",
    )(role, mixed, mixed, grad, grad, gated, gated, gain, gain, mean, inv)


def fold_slots(vg_ref, acc_ref, bands, last_band):
    for e in bands:
        at = (last_band - e) * PAIR
        for a in range(2):
            for b in range(2):
                slot = 2 * e + a - b
                if slot < 0 or slot >= BAND_BLOCKS or a == 1 and b == 1:
                    continue
                value = vg_ref[a * 128:(a + 1) * 128, at + b * 128:at + (b + 1) * 128]
                if a == b:
                    value = value + vg_ref[128:, at + 128:at + 256]
                rows = slice(slot * 128, (slot + 1) * 128)
                acc_ref[rows, :] = acc_ref[rows, :] + value


def local_body(role, m, g, u, n, mean_ref, inv_ref, v_ref, vt_ref, mo, no, acc, vg, a_s, d_s, bias):
    step = pl.program_id(0)

    @pl.when(step == 0)
    def _():
        vg[...] = jnp.zeros_like(vg)
        bias[...] = jnp.zeros_like(bias)
        acc[...] = jnp.zeros_like(acc)

    width = m.shape[1]
    for p in range(3):
        rows = slice(p * PAIR, (p + 1) * PAIR)
        hat = hat_of(m[rows, :], mean_ref[rows, :], inv_ref[rows, :])
        a_s[p] = (hat * n[...]).astype(BF16)
        d_s[p] = (g[rows, :].astype(F32) * u[rows, :].astype(F32)).astype(BF16)
    ones = jnp.ones((8, width), BF16)
    gain = jnp.zeros((1, width), F32)
    a_all = a_s[...].reshape(3 * PAIR, width)
    d_all = d_s[...].reshape(3 * PAIR, width)
    for p in range(3):
        rows = slice(p * PAIR, (p + 1) * PAIR)
        mixed = dot(v_ref[:, (2 - p) * PAIR:], a_all[:(p + 1) * PAIR])
        dnorm = dot(vt_ref[:, :(3 - p) * PAIR], d_all[p * PAIR:])
        at = (2 - p) * PAIR
        vg[:, at:] = vg[:, at:] + nt_dot(d_s[p], a_all[:(p + 1) * PAIR])
        mo[rows, :] = mixed.astype(BF16)
        no[rows, :] = dnorm.astype(BF16)
        gain = gain + jnp.sum(dnorm * a_s[p].astype(F32), axis=0, keepdims=True)
    bias[...] = bias[...] + nt_dot(ones, d_all)
    gain = gain / n[...]
    for k in range(width // 128):
        acc[pl.ds(SLOT_ROWS + step * (width // 128) + k, 1), :] = gain[:, k * 128:(k + 1) * 128]

    @pl.when(step == pl.num_programs(0) - 1)
    def _():
        fold_slots(vg, acc, range(3), 2)
        row = lax.broadcasted_iota(jnp.int32, (128, 128), 0)
        col = lax.broadcasted_iota(jnp.int32, (128, 128), 1)
        acc[:128, :] = jnp.where(row >= col, acc[:128, :], 0.0)
        for k in range(6):
            acc[pl.ds(SLOT_ROWS + GAIN_ROWS + role[0] * 6 + k, 1), :] = bias[0:1, k * 128:(k + 1) * 128]


def local_part(role, mixed, grad, gated, gain, mean, inv, v, vt):
    tokens, full = mixed.shape
    width = 512
    block = pl.BlockSpec((tokens, width), lambda j, r: (0, j))
    col = pl.BlockSpec((tokens, 128), lambda j, r: (0, 0))
    down = pl.BlockSpec((PAIR, 3 * PAIR), lambda j, r: (0, BANDS // 3 - 1))
    up = pl.BlockSpec((PAIR, 3 * PAIR), lambda j, r: (0, 0))
    return pl.pallas_call(
        local_body,
        grid_spec=pltpu.PrefetchScalarGridSpec(
            num_scalar_prefetch=1,
            grid=(full // width,),
            in_specs=[block, block, block, pl.BlockSpec((1, width), lambda j, r: (0, j)), col, col, down, up],
            out_specs=[block, block, pl.BlockSpec((ACC_ROWS, 128), lambda j, r: (0, 0))],
            scratch_shapes=[
                pltpu.VMEM((PAIR, 3 * PAIR), F32),
                pltpu.VMEM((3, PAIR, width), BF16),
                pltpu.VMEM((3, PAIR, width), BF16),
                pltpu.VMEM((8, tokens), F32),
            ],
        ),
        out_shape=[
            jax.ShapeDtypeStruct((tokens, full), BF16),
            jax.ShapeDtypeStruct((tokens, full), BF16),
            jax.ShapeDtypeStruct((ACC_ROWS, 128), F32),
        ],
        compiler_params=params(),
        name="local_part",
    )(role, mixed, grad, gated, gain, mean, inv, v, vt)


def owner_body(kind, width, first, second):
    mine = (0, 3) if kind == "z" else (1, 2)

    def body(role, cols, own, r0, r1, r2, gain_ref, v_in, vt_in, s_in, st_in, acc_in,
             o0, o1, o2, o3, acc_out,
             a_s, d_s, m_f, n_f, m_s, n_s, vg, sg, acc_s, v_ref, vt_ref, s_ref, st_ref, in_sem, acc_sem, m_sem, n_sem, t_sem):
        r = role[0]

        def third(buf, k):
            return buf.at[pl.ds(6 * k, 6)]

        mine_x, mine_y = own.at[0], own.at[1]
        if kind == "z":
            sources = {
                0: (mine_x, r0.at[0], r1.at[0], r0.at[1], r1.at[1], r2),
                3: (r2, r1.at[0], r0.at[0], r1.at[1], r0.at[1], mine_x),
            }
            targets = {
                0: ((o0.at[0], o1.at[0], o2), (o3, o0.at[1], o1.at[1])),
                3: ((o1.at[0], o0.at[0], o3), (o2, o1.at[1], o0.at[1])),
            }
        else:
            sources = {
                1: (r0, mine_x, r2.at[0], mine_y, r2.at[1], r1),
                2: (r1, r2.at[0], mine_x, r2.at[1], mine_y, r0),
            }
            targets = {
                1: ((o3.at[0], o2.at[0], o1), (o0, o3.at[1], o2.at[1])),
                2: ((o2.at[0], o3.at[0], o0), (o1, o2.at[1], o3.at[1])),
            }
        places = [third(a_s, 0), third(a_s, 1), third(a_s, 2), third(d_s, 0), third(d_s, 1), third(d_s, 2)]

        @pl.when((r == mine[0]) | (r == mine[1]))
        def _():
            fetch = pltpu.make_async_copy(acc_in, acc_s, acc_sem)
            fetch.start()
            for who in mine:
                @pl.when(r == who)
                def _():
                    copies = [
                        pltpu.make_async_copy(src, dst, in_sem.at[k])
                        for k, (src, dst) in enumerate(zip(sources[who], places))
                    ]
                    for copy in copies:
                        copy.start()
            loads = [
                pltpu.make_async_copy(src, dst, t_sem.at[k])
                for k, (src, dst) in enumerate(((v_in, v_ref), (vt_in, vt_ref), (s_in, s_ref), (st_in, st_ref)))
            ]
            for load in loads:
                load.start()
            vg[...] = jnp.zeros_like(vg)
            sg[...] = jnp.zeros_like(sg)
            m_f[:4] = jnp.zeros((4, 128, width), F32)
            n_f[...] = jnp.zeros_like(n_f)
            for k in range(6):
                pltpu.make_async_copy(mine_x, places[k], in_sem.at[k]).wait()
            for load in loads:
                load.wait()

            def pair(buf, p):
                return buf[pl.ds(2 * p, 2)].reshape(PAIR, width)

            def strided(i, carry):
                c0 = cols[BAND_BLOCKS + i, 0]
                c1 = cols[BAND_BLOCKS + i, 1]
                picked = jnp.concatenate([a_s[c0], a_s[c1]], axis=0)
                dmix = d_s[10 + i]
                m_f[4 + i] = dot(s_ref[...], picked)
                back = dot(st_ref[...], dmix)
                n_f[c0] = n_f[c0] + back[:128]
                n_f[c1] = n_f[c1] + back[128:]
                sg[...] = sg[...] + nt_dot(dmix, picked)
                return carry

            lax.fori_loop(0, 8, strided, 0)

            for dev in range(1, 4):
                low = 1 if dev == 3 else 0
                count = 3 * dev - low

                def forward(t, carry):
                    g = 3 * (dev - 1) + t
                    at = pl.ds(pl.multiple_of((BANDS - 1 - 3 * dev + low - t) * PAIR, PAIR), count * PAIR)
                    normed = a_s[2 * low:6 * dev].reshape(count * PAIR, width)
                    total = dot(v_ref[:, at], normed)
                    if dev > 1:
                        total = total + pair(m_f, g - 3)
                    m_s[pl.ds(2 * g, 2)] = total.astype(BF16).reshape(2, 128, width)
                    vg[:, at] = vg[:, at] + nt_dot(pair(d_s, g), normed)
                    return carry

                lax.fori_loop(0, 3, forward, 0)

            for who in mine:
                @pl.when(r == who)
                def _():
                    for k in range(3):
                        pltpu.make_async_copy(third(m_s, k), targets[who][0][k], m_sem.at[k]).start()

            total_gain = jnp.zeros((1, width), F32)
            for dev in range(3):
                count = 8 if dev == 0 else 9 - 3 * dev

                def backward(t, gain):
                    p = 3 * dev + t
                    at = pl.ds(pl.multiple_of((3 - t) * PAIR, PAIR), count * PAIR)
                    dmix = d_s[6 * dev:6 * dev + 2 * count].reshape(count * PAIR, width)
                    total = dot(vt_ref[:, at], dmix)
                    if dev < 2:
                        total = total + pair(n_f, p)
                    n_s[pl.ds(2 * p, 2)] = total.astype(BF16).reshape(2, 128, width)
                    return gain + jnp.sum(total * pair(a_s, p).astype(F32), axis=0, keepdims=True)

                total_gain = lax.fori_loop(0, 3, backward, total_gain)
            total_gain = total_gain / gain_ref[...]
            fetch.wait()
            base = jnp.where(r == mine[0], first, second) // 128
            for k in range(width // 128):
                where = pl.ds(SLOT_ROWS + base + k, 1)
                acc_s[where, :] = acc_s[where, :] + total_gain[:, k * 128:(k + 1) * 128]

            for who in mine:
                @pl.when(r == who)
                def _():
                    for k in range(3):
                        pltpu.make_async_copy(third(n_s, k), targets[who][1][k], n_sem.at[k]).start()

            fold_slots(vg, acc_s, range(1, 9), BANDS - 1)
            for s in range(NSTR):
                rows = slice((BAND_BLOCKS + s) * 128, (BAND_BLOCKS + s + 1) * 128)
                acc_s[rows, :] = acc_s[rows, :] + sg[:, s * 128:(s + 1) * 128]
            put = pltpu.make_async_copy(acc_s, acc_out, acc_sem)
            put.start()
            some = o2 if kind == "z" else o0
            for k in range(3):
                pltpu.make_async_copy(third(m_s, k), some, m_sem.at[k]).wait()
                pltpu.make_async_copy(third(n_s, k), some, n_sem.at[k]).wait()
            put.wait()

    return body


def owner(kind, first, second, width, role, cols, own, received, gain, tables, acc):
    hbm = pl.BlockSpec(memory_space=pl.ANY)
    v, vt, s, st = tables
    mine = (0, 3) if kind == "z" else (1, 2)

    def gain_at(i, r, c):
        return (0, jnp.where(r[0] == mine[1], second, first) // width)

    one = jax.ShapeDtypeStruct((6, 128, width), BF16)
    two = jax.ShapeDtypeStruct((2, 6, 128, width), BF16)
    return pl.pallas_call(
        owner_body(kind, width, first, second),
        grid_spec=pltpu.PrefetchScalarGridSpec(
            num_scalar_prefetch=2,
            grid=(1,),
            in_specs=[hbm] * 4
            + [pl.BlockSpec((1, width), gain_at)] + [hbm] * 5,
            out_specs=[hbm] * 5,
            scratch_shapes=[
                pltpu.VMEM((18, 128, width), BF16),
                pltpu.VMEM((18, 128, width), BF16),
                pltpu.VMEM((12, 128, width), F32),
                pltpu.VMEM((12, 128, width), F32),
                pltpu.VMEM((18, 128, width), BF16),
                pltpu.VMEM((18, 128, width), BF16),
                pltpu.VMEM((PAIR, BANDS * PAIR), F32),
                pltpu.VMEM((128, PAIR), F32),
                pltpu.VMEM((ACC_ROWS, 128), F32),
                pltpu.VMEM(v.shape, BF16),
                pltpu.VMEM(vt.shape, BF16),
                pltpu.VMEM(s.shape, BF16),
                pltpu.VMEM(st.shape, BF16),
                pltpu.SemaphoreType.DMA((6,)),
                pltpu.SemaphoreType.DMA,
                pltpu.SemaphoreType.DMA((3,)),
                pltpu.SemaphoreType.DMA((3,)),
                pltpu.SemaphoreType.DMA((4,)),
            ],
        ),
        out_shape=([two, two, one, one] if kind == "z" else [one, one, two, two])
        + [jax.ShapeDtypeStruct((ACC_ROWS, 128), F32)],
        input_output_aliases={11: 4},
        compiler_params=params(),
    )(role, cols, own, *received, gain, v, vt, s, st, acc)


def absorb(first, second, width, role, mixed, grad, m_loc, n_loc, gain, mean, bias, pieces, carried):
    tokens, full = mixed.shape
    steps = width // SEG

    def at(j, r):
        left = jnp.where(r[0] < 2, first, second) // SEG
        right = jnp.where(r[0] < 2, second, first) // SEG
        return jnp.where(j < steps, left + j, right + j - steps)

    begins = carried is None

    def body(role, m, g, ml, nl, n, mean_ref, bias_ref, single_a, both_a, single_b, both_b, *rest):
        gated_out, grad_out, sums = rest[-3:]
        j = pl.program_id(0)
        r = role[0]
        edge = (r == 0) | (r == 3)

        @pl.when(j == 0)
        def _():
            sums[...] = jnp.zeros_like(sums) if begins else rest[2][...]

        def take(find):
            for i in range(6):
                rows = slice(i * 128, (i + 1) * 128)
                off_m, off_n = find(i)
                mean, bias = mean_ref[rows, :], bias_ref[rows, :]
                one, two = sums[0, rows, :], sums[1, rows, :]
                for k in range(0, SEG, 128):
                    lanes = slice(k, k + 128)
                    total = (off_m[:, lanes] + ml[rows, lanes].astype(F32) + bias).astype(BF16).astype(F32)
                    gated_out[rows, lanes] = (g[rows, lanes].astype(F32) * total).astype(BF16)
                    dnorm = (off_n[:, lanes] + nl[rows, lanes].astype(F32)).astype(BF16)
                    grad_out[rows, lanes] = dnorm
                    hat_grad = dnorm.astype(F32) * n[:, lanes]
                    one = one + hat_grad
                    two = two + hat_grad * (m[rows, lanes].astype(F32) - mean)
                sums[0, rows, :] = one
                sums[1, rows, :] = two

        for half, single, both in ((j < steps, single_a, both_a), (j >= steps, single_b, both_b)):
            @pl.when(half & edge)
            def _():
                def find(i):
                    one = single[i].astype(F32)
                    return jnp.where(r == 3, one, 0.0), jnp.where(r == 0, one, 0.0)

                take(find)

            @pl.when(half & jnp.logical_not(edge))
            def _():
                take(lambda i: (both[0, i].astype(F32), both[1, i].astype(F32)))

    block = pl.BlockSpec((tokens, SEG), lambda j, r: (0, at(j, r)))
    line = pl.BlockSpec((1, SEG), lambda j, r: (0, at(j, r)))
    col = pl.BlockSpec((tokens, 128), lambda j, r: (0, 0))

    def single_at(j, r):
        return jnp.where((r[0] == 0) | (r[0] == 3), j, 0)

    def both_at(j, r):
        return jnp.where((r[0] == 0) | (r[0] == 3), 0, j)

    one_a = pl.BlockSpec((6, 128, SEG), lambda j, r: (0, 0, single_at(jnp.minimum(j, steps - 1), r)))
    two_a = pl.BlockSpec((2, 6, 128, SEG), lambda j, r: (0, 0, 0, both_at(jnp.minimum(j, steps - 1), r)))
    one_b = pl.BlockSpec((6, 128, SEG), lambda j, r: (0, 0, single_at(jnp.maximum(j - steps, 0), r)))
    two_b = pl.BlockSpec((2, 6, 128, SEG), lambda j, r: (0, 0, 0, both_at(jnp.maximum(j - steps, 0), r)))
    hbm = pl.BlockSpec(memory_space=pl.ANY)
    total = pl.BlockSpec((2, tokens, 128), lambda j, r: (0, 0, 0))
    return pl.pallas_call(
        body,
        grid_spec=pltpu.PrefetchScalarGridSpec(
            num_scalar_prefetch=1,
            grid=(2 * steps,),
            in_specs=[block] * 4 + [line, col, col, one_a, two_a, one_b, two_b] + ([] if begins else [hbm, hbm, total]),
            out_specs=[block, block, total],
        ),
        out_shape=[
            jax.ShapeDtypeStruct((tokens, full), BF16),
            jax.ShapeDtypeStruct((tokens, full), BF16),
            jax.ShapeDtypeStruct((2, tokens, 128), F32),
        ],
        input_output_aliases={} if begins else {12: 0, 13: 1, 14: 2},
        compiler_params=params(),
    )(role, mixed, grad, m_loc, n_loc, gain, mean, bias, *pieces, *(carried or ()))


def finish_body(m, d, n, mean_ref, inv_ref, sums, value_out):
    full = m.shape[1]
    inv = inv_ref[...]
    mean = mean_ref[...]
    shift = jnp.sum(sums[0], axis=1, keepdims=True) * (1.0 / full) * inv
    slope = jnp.sum(sums[1], axis=1, keepdims=True) * (1.0 / full) * inv * inv * inv
    for k in range(0, full, 128):
        at = slice(k, k + 128)
        value = d[:, at].astype(F32) * n[:, at] * inv - shift - (m[:, at].astype(F32) - mean) * slope
        value_out[:, at] = value.astype(BF16)


def finish(mixed, dnorm, gain, mean, inv, sums):
    tokens, full = mixed.shape
    rows = 192
    row = pl.BlockSpec((rows, full), lambda i: (i, 0))
    col = pl.BlockSpec((rows, 128), lambda i: (i, 0))
    return pl.pallas_call(
        finish_body,
        grid=(tokens // rows,),
        in_specs=[row, row, pl.BlockSpec((1, full), lambda i: (0, 0)), col, col, pl.BlockSpec((2, rows, 128), lambda i: (0, i, 0))],
        out_specs=row,
        out_shape=jax.ShapeDtypeStruct((tokens, full), BF16),
        compiler_params=params(),
        name="finish",
    )(mixed, dnorm, gain, mean, inv, sums)


def move(value, pairs):
    return lax.ppermute(value, "seq", pairs)


def backwards(pairs):
    return tuple((b, a) for a, b in pairs)


def sum_over_all(acc):
    dp, seq = lax.axis_size("dp"), lax.axis_size("seq")

    def exchange(value, axis):
        return lax.all_to_all(value, axis, 0, 0, tiled=True)

    part = jnp.sum(exchange(acc.reshape(dp, -1, 128), "dp"), axis=0).reshape(seq, -1, 128)
    part = jnp.sum(exchange(part, "seq"), axis=0).astype(BF16)
    part = exchange(jnp.broadcast_to(part, (seq,) + part.shape), "seq").reshape(-1, 128)
    part = exchange(jnp.broadcast_to(part, (dp,) + part.shape), "dp").reshape(-1, 128)
    return part.astype(F32)


def shards_of_four(gated_part, mixed_part, out_grad, norm_gain, mix_bias, token_mixing_weight, stride_cols):
    return four(gated_part, mixed_part, out_grad, norm_gain, mix_bias, token_mixing_weight, stride_cols)


def four(gated_part, mixed_part, out_grad, norm_gain, mix_bias, token_mixing_weight, stride_cols):
    batch_size = lax.axis_size("dp")
    seq_parts = lax.axis_size("seq")
    gated, mixed, grad = gated_part[0], mixed_part[0], out_grad[0]
    tokens, full = mixed.shape
    index = lax.axis_index("seq").astype(jnp.int32)
    role = index.reshape(1)
    gain = norm_gain.reshape(1, full)
    starts = segment_starts()
    mean, inv = stats(mixed)
    packed, received = {}, {}
    for key in ORDER:
        kind = key[0]
        packed[key] = pack(kind, role, mixed, grad, gated, gain, mean, inv, *starts[key])
        a, b, c = packed[key][:3]
        xs, ys, ds = X_PAIRS[kind], Y_PAIRS[kind], D_PAIRS[kind]
        if kind == "z":
            received[key] = (move(a, xs), move(b, ys), move(c, ds))
        else:
            received[key] = (move(packed[key][3], xs), move(c, ys), move(b, ds))
    tables = prep(token_mixing_weight)
    m_loc, n_loc, acc = local_part(role, mixed, grad, gated, gain, mean, inv, tables[0], tables[1])
    back = {}
    for key in ORDER:
        kind = key[0]
        first, second, width = starts[key]
        *out, acc = owner(kind, first, second, width, role, stride_cols, packed[key][0], received[key], gain, tables, acc)
        xs, ys, ds = backwards(X_PAIRS[kind]), backwards(Y_PAIRS[kind]), D_PAIRS[kind]
        to_x = move(out[0], xs)
        to_y = move(out[1], ys)
        far = move(out[2], ds)
        back[key] = (out[3], to_x, far, to_y) if kind == "z" else (to_x, out[3], to_y, far)
    total = sum_over_all(acc)
    bias_col = lax.dynamic_slice_in_dim(mix_bias, index * tokens, tokens, 0)
    bias_col = jnp.broadcast_to(bias_col[:, None], (tokens, 128))
    carried = None
    for key in ORDER:
        kind = key[0]
        carried = absorb(*starts[key], role, mixed, grad, m_loc, n_loc, gain, mean, bias_col, back[key], carried)
    gated_grad, dnorm, sums = carried
    value_grad = finish(mixed, dnorm, gain, mean, inv, sums)
    total_len = tokens * seq_parts
    weight_grad = total[:SLOT_ROWS].reshape(18, 128, 128) / math.sqrt(batch_size * total_len * full)
    gain_grad = total[SLOT_ROWS:SLOT_ROWS + GAIN_ROWS].reshape(full) / math.sqrt(batch_size * total_len)
    bias_rows = lax.dynamic_slice_in_dim(total, SLOT_ROWS + GAIN_ROWS + index * 6, 6, 0).reshape(tokens)
    bias_grad = bias_rows / math.sqrt(batch_size * full)
    return (gated_grad[None], value_grad[None], weight_grad, gain_grad, bias_grad)


def solution(mesh):
    placed = (P("dp", "seq", None), P("dp", "seq", None), P("dp", "seq", None), P(), P(), P(), P())
    small = mesh.shape["seq"] == 4
    return jax.shard_map(
        shards_of_four if small else shards,
        mesh=mesh,
        in_specs=placed,
        out_specs=(P("dp", "seq", None), P("dp", "seq", None), P(), P(), P("seq")),
        check_vma=False,
    )
```

```python
import math

import jax
import jax.numpy as jnp
from jax import lax
from jax.experimental import pallas as pl
from jax.experimental.pallas import tpu as pltpu
from jax.sharding import PartitionSpec as P


MIXING_BLOCK = 128
BAND_BLOCKS = 16
NSTR = 2


EPS = 1e-05


def slot_mask(shape):
    slot_idx = lax.broadcasted_iota(jnp.int32, shape, 0)
    row_idx = lax.broadcasted_iota(jnp.int32, shape, 1)
    col_idx = lax.broadcasted_iota(jnp.int32, shape, 2)
    return (slot_idx > 0) | (row_idx >= col_idx)


def band_matrix(weights, backward):
    group = 2
    columns = group + BAND_BLOCKS - 1
    row_ids = jnp.arange(group, dtype=jnp.int32)[:, None]
    col_ids = jnp.arange(columns, dtype=jnp.int32)[None, :]
    if backward:
        offsets = col_ids - row_ids
    else:
        offsets = row_ids + BAND_BLOCKS - 1 - col_ids
    valid = (offsets >= 0) & (offsets < BAND_BLOCKS)
    clipped = jnp.clip(offsets, 0, BAND_BLOCKS - 1)
    tiles = jnp.take(weights[:BAND_BLOCKS], clipped.reshape(-1), axis=0)
    tiles = tiles.reshape(group, columns, MIXING_BLOCK, MIXING_BLOCK)
    if backward:
        tiles = jnp.swapaxes(tiles, 2, 3)
    tiles = jnp.where(valid[:, :, None, None], tiles, jnp.zeros((), tiles.dtype))
    return tiles.transpose(0, 2, 1, 3).reshape(group * MIXING_BLOCK, columns * MIXING_BLOCK)


def band_apply(matrix, padded, num_blocks, width):
    group = 2
    span_len = (group + BAND_BLOCKS - 1) * MIXING_BLOCK

    def one_group(group_id):
        piece = lax.dynamic_slice_in_dim(padded, group_id * group * MIXING_BLOCK, span_len, 0)
        return jnp.dot(matrix, piece, preferred_element_type=jnp.float32)

    result = lax.map(one_group, jnp.arange(num_blocks // group, dtype=jnp.int32))
    return result.reshape(num_blocks, MIXING_BLOCK, width)


def strided_blocks(blocks, stride_cols, strided):
    valid_rows = stride_cols[:, strided] >= 0
    safe_cols = jnp.maximum(stride_cols[:, strided], 0)
    picked = jnp.take(blocks, safe_cols, axis=0)
    return (
        jnp.where(valid_rows[:, None, None], picked, jnp.zeros((), picked.dtype)),
        valid_rows,
        safe_cols,
    )


def mix_forward(blocks, weights, stride_cols, mix_bias):
    num_blocks, _, width = blocks.shape
    tokens = blocks.reshape(num_blocks * MIXING_BLOCK, width)
    front = jnp.zeros(((BAND_BLOCKS - 1) * MIXING_BLOCK, width), blocks.dtype)
    padded = jnp.concatenate([front, tokens], axis=0)
    mixed_sum = band_apply(band_matrix(weights, False), padded, num_blocks, width)
    for strided in range(NSTR):
        picked, _, _ = strided_blocks(blocks, stride_cols, strided)
        mixed_sum = mixed_sum + jnp.einsum(
            "ab,nbc->nac",
            weights[BAND_BLOCKS + strided],
            picked,
            preferred_element_type=jnp.float32,
        )
    mixed_sum = mixed_sum + mix_bias.reshape(num_blocks, MIXING_BLOCK, 1)
    return (mixed_sum.astype(jnp.bfloat16), padded)


def mix_backward(dblocks, blocks, padded, weights, stride_cols):
    num_blocks, _, width = blocks.shape
    total_len = num_blocks * MIXING_BLOCK
    dtokens = dblocks.reshape(total_len, width)
    tail = jnp.zeros(((BAND_BLOCKS - 1) * MIXING_BLOCK, width), dblocks.dtype)
    padded_back = jnp.concatenate([dtokens, tail], axis=0)
    dnorm = band_apply(band_matrix(weights, True), padded_back, num_blocks, width)
    band_grads = []
    for offset in range(BAND_BLOCKS):
        start = (BAND_BLOCKS - 1 - offset) * MIXING_BLOCK
        shifted = lax.slice_in_dim(padded, start, start + total_len, axis=0).reshape(
            num_blocks, MIXING_BLOCK, width
        )
        band_grads.append(
            jnp.einsum("nac,nbc->ab", dblocks, shifted, preferred_element_type=jnp.float32)
        )
    far_grads = []
    block_ids = jnp.arange(num_blocks, dtype=jnp.int32)
    for strided in range(NSTR):
        picked, valid_rows, safe_cols = strided_blocks(blocks, stride_cols, strided)
        far_grads.append(
            jnp.einsum("nac,nbc->ab", dblocks, picked, preferred_element_type=jnp.float32)
        )
        scatter_term = jnp.einsum(
            "ab,nac->nbc",
            weights[BAND_BLOCKS + strided],
            dblocks,
            preferred_element_type=jnp.float32,
        )
        scatter_term = jnp.where(
            valid_rows[:, None, None], scatter_term, jnp.zeros((), jnp.float32)
        )
        one_hot = (block_ids[:, None] == safe_cols[None, :]).astype(jnp.float32)
        dnorm = dnorm + jnp.einsum(
            "ji,ibc->jbc", one_hot, scatter_term, precision=lax.Precision.HIGHEST
        )
    slot_grad = jnp.stack(band_grads + far_grads)
    slot_grad = jnp.where(slot_mask(slot_grad.shape), slot_grad, jnp.zeros((), jnp.float32))
    return (dnorm.astype(jnp.bfloat16), slot_grad)


def shards(gated_part, mixed_part, out_grad, norm_gain, mix_bias, token_mixing_weight, stride_cols):
    seq_parts = lax.axis_size("seq")
    batch_size = lax.axis_size("dp")
    gated_rows = gated_part[0]
    value_rows = mixed_part[0]
    grad_rows = out_grad[0]
    tok_local, half_width = gated_rows.shape
    slice_width = half_width // seq_parts
    total_len = tok_local * seq_parts
    num_blocks = total_len // MIXING_BLOCK
    values = value_rows.astype(jnp.float32)
    row_mean = jnp.mean(values, axis=1, keepdims=True)
    centered = values - row_mean
    row_var = jnp.mean(centered * centered, axis=1, keepdims=True)
    inv_std = lax.rsqrt(row_var + EPS)
    norm_hat = centered * inv_std
    normed = (norm_hat * norm_gain).astype(jnp.bfloat16)
    weights = jnp.where(
        slot_mask(token_mixing_weight.shape),
        token_mixing_weight,
        jnp.zeros((), token_mixing_weight.dtype),
    )

    def to_panels(rows):
        return rows.reshape(tok_local, seq_parts, slice_width)

    def to_blocks(panel):
        return panel.reshape(num_blocks, MIXING_BLOCK, slice_width)

    def to_columns(blocks):
        return blocks.reshape(total_len, 1, slice_width)

    panel_norm = lax.all_to_all(to_panels(normed), "seq", split_axis=1, concat_axis=0, tiled=True)
    blocks = to_blocks(panel_norm)
    mixed16, padded = mix_forward(blocks, weights, stride_cols, mix_bias)
    mixed_rows = lax.all_to_all(
        to_columns(mixed16), "seq", split_axis=0, concat_axis=1, tiled=True
    ).reshape(tok_local, half_width)
    grad_f32 = grad_rows.astype(jnp.float32)
    gated_grad_rows = (grad_f32 * mixed_rows.astype(jnp.float32)).astype(jnp.bfloat16)
    dmix16 = (grad_f32 * gated_rows.astype(jnp.float32)).astype(jnp.bfloat16)
    local_bias = jnp.sum(dmix16.astype(jnp.float32), axis=1)
    bias_rows = lax.psum(local_bias, "dp")
    panel_dmix = lax.all_to_all(to_panels(dmix16), "seq", split_axis=1, concat_axis=0, tiled=True)
    dnorm16, slot_grad = mix_backward(to_blocks(panel_dmix), blocks, padded, weights, stride_cols)
    dnorm_rows = lax.all_to_all(
        to_columns(dnorm16), "seq", split_axis=0, concat_axis=1, tiled=True
    ).reshape(tok_local, half_width)
    dnorm_f32 = dnorm_rows.astype(jnp.float32)
    hat_grad = dnorm_f32 * norm_gain
    value_grad = inv_std * (
        hat_grad
        - jnp.mean(hat_grad, axis=1, keepdims=True)
        - norm_hat * jnp.mean(hat_grad * norm_hat, axis=1, keepdims=True)
    )
    gain_part = jnp.sum(dnorm_f32 * norm_hat, axis=0)
    slot_sum, gain_sum = lax.psum((slot_grad, gain_part), ("dp", "seq"))
    weight_grad = slot_sum / math.sqrt(batch_size * total_len * half_width)
    gain_grad = gain_sum / math.sqrt(batch_size * total_len)
    bias_grad = bias_rows / math.sqrt(batch_size * half_width)
    return (
        gated_grad_rows[None],
        value_grad.astype(jnp.bfloat16)[None],
        weight_grad,
        gain_grad,
        bias_grad,
    )


PAIR = 2 * MIXING_BLOCK
BANDS = 12
Z_CHUNKS = (512, 512, 256)
O_CHUNKS = (768,)
ORDER = (("z", 0), ("o", 0), ("z", 1), ("z", 2))
X_PAIRS = {"z": ((1, 0), (2, 3)), "o": ((0, 1), (3, 2))}
Y_PAIRS = {"z": ((2, 0), (1, 3)), "o": ((0, 2), (3, 1))}
D_PAIRS = {"z": ((0, 3), (3, 0)), "o": ((1, 2), (2, 1))}
SLOT_ROWS = 18 * 128
GAIN_ROWS = 32
ACC_ROWS = 2560
F32 = jnp.float32
BF16 = jnp.bfloat16


def segment_starts():
    table = {}
    at = 0
    for width in sorted(set(Z_CHUNKS + O_CHUNKS), reverse=True):
        for kind, chunks in (("z", Z_CHUNKS), ("o", O_CHUNKS)):
            for number, chunk in enumerate(chunks):
                if chunk == width:
                    table[kind, number] = (at, at + width, width)
                    at += 2 * width
    return table


LIMITS = {"prep": 12, "stats": 24, "pack": 20, "local": 32, "owner": 48, "absorb": 32, "finish": 24}


def params(kernel, **kw):
    limit = LIMITS[kernel]
    return pltpu.CompilerParams(vmem_limit_bytes=limit * 1024 * 1024, **kw)


def nt_dot(left, right):
    return lax.dot_general(left, right, (((1,), (1,)), ((), ())), preferred_element_type=F32)


def dot(left, right):
    return jnp.dot(left, right, preferred_element_type=F32)


def prep_body(w_ref, v_ref, vt_ref, s_ref, st_ref):
    row = lax.broadcasted_iota(jnp.int32, (128, 128), 0)
    col = lax.broadcasted_iota(jnp.int32, (128, 128), 1)
    zero = jnp.zeros((128, 128), BF16)

    def block(slot):
        if slot < 0 or slot >= BAND_BLOCKS:
            return zero, zero
        value = w_ref[slot].astype(F32)
        if slot == 0:
            value = jnp.where(row >= col, value, 0.0)
        return value.astype(BF16), value.T.astype(BF16)

    for e in range(BANDS):
        for a in range(2):
            for b in range(2):
                value, turned = block(2 * e + a - b)
                down = (BANDS - 1 - e) * PAIR
                v_ref[a * 128:(a + 1) * 128, down + b * 128:down + (b + 1) * 128] = value
                vt_ref[b * 128:(b + 1) * 128, e * PAIR + a * 128:e * PAIR + (a + 1) * 128] = turned
    for s in range(NSTR):
        value = w_ref[BAND_BLOCKS + s]
        s_ref[:, s * 128:(s + 1) * 128] = value
        st_ref[s * 128:(s + 1) * 128, :] = value.astype(F32).T.astype(BF16)


def prep(weights):
    return pl.pallas_call(
        prep_body,
        out_shape=(
            jax.ShapeDtypeStruct((PAIR, BANDS * PAIR), BF16),
            jax.ShapeDtypeStruct((PAIR, BANDS * PAIR), BF16),
            jax.ShapeDtypeStruct((128, PAIR), BF16),
            jax.ShapeDtypeStruct((PAIR, 128), BF16),
        ),
        compiler_params=params("prep"),
        name="prep",
    )(weights)


def lanes_of(width):
    return [slice(k, k + 128) for k in range(0, width, 128)]


def some_rows(i, count=16):
    return pl.ds(pl.multiple_of(i * count, count), count)


def stats_body(v_ref, mean_ref, inv_ref):
    values = v_ref[...].astype(F32)
    mean = jnp.mean(values, axis=1, keepdims=True)
    centered = values - mean
    var = jnp.mean(centered * centered, axis=1, keepdims=True)
    mean_ref[...] = jnp.broadcast_to(mean, mean_ref.shape)
    inv_ref[...] = jnp.broadcast_to(lax.rsqrt(var + EPS), inv_ref.shape)


def stats(value_rows):
    tokens, width = value_rows.shape
    rows = 192
    col = pl.BlockSpec((rows, 128), lambda i: (i, 0))
    return pl.pallas_call(
        stats_body,
        grid=(tokens // rows,),
        in_specs=[pl.BlockSpec((rows, width), lambda i: (i, 0))],
        out_specs=[col, col],
        out_shape=[jax.ShapeDtypeStruct((tokens, 128), F32)] * 2,
        compiler_params=params("stats"),
        name="stats",
    )(value_rows)


def hat_of(m, mean, inv):
    parts = [(m[:, k:k + 128].astype(F32) - mean) * inv for k in range(0, m.shape[1], 128)]
    return jnp.concatenate(parts, axis=1)


def pack_body(kind):
    def body(role, ma, mb, ga, gb, ua, ub, na, nb, mean_ref, inv_ref, a_out, b_out, c_out, *more):
        last = role[0] == 3
        half = pl.program_id(0) * (384 // 16)

        def group(i, carry):
            at = some_rows(i)
            block, inside = i // 8, some_rows(i % 8)
            mean, inv = mean_ref[some_rows(half + i), :], inv_ref[some_rows(half + i), :]
            for side, (m, g, u, n) in enumerate(((ma, ga, ua, na), (mb, gb, ub, nb))):
                out = b_out if side else a_out
                for lane in lanes_of(m.shape[1]):
                    normed = (m[at, lane].astype(F32) - mean) * inv * n[:, lane]
                    dmix = g[at, lane].astype(F32) * u[at, lane].astype(F32)
                    x = jnp.where(last, dmix, normed).astype(BF16)
                    out[0, block, inside, lane] = x
                    out[1, block, inside, lane] = jnp.where(last, normed, dmix).astype(BF16)
                    if side == 1:
                        c_out[block, inside, lane] = x
                    elif kind == "o":
                        more[0][block, inside, lane] = x
            return carry

        lax.fori_loop(0, 384 // 16, group, 0)

    return body


def pack(kind, role, mixed, grad, gated, gain, mean, inv, first, second, width):
    tokens = mixed.shape[0]

    def left(r):
        return jnp.where(r[0] < 2, first, second) // width

    def right(r):
        return jnp.where(r[0] < 2, second, first) // width

    main = [pl.BlockSpec((384, width), lambda i, r: (i, left(r))), pl.BlockSpec((384, width), lambda i, r: (i, right(r)))]
    line = [pl.BlockSpec((1, width), lambda i, r: (0, left(r))), pl.BlockSpec((1, width), lambda i, r: (0, right(r)))]
    col = pl.BlockSpec((tokens, 128), lambda i, r: (0, 0))
    two = pl.BlockSpec((2, 3, 128, width), lambda i, r: (0, i, 0, 0))
    one = pl.BlockSpec((3, 128, width), lambda i, r: (i, 0, 0))
    count = 2 if kind == "o" else 1
    return pl.pallas_call(
        pack_body(kind),
        grid_spec=pltpu.PrefetchScalarGridSpec(
            num_scalar_prefetch=1,
            grid=(tokens // 384,),
            in_specs=main * 3 + line + [col, col],
            out_specs=[two, two] + [one] * count,
        ),
        out_shape=[jax.ShapeDtypeStruct((2, 6, 128, width), BF16)] * 2
        + [jax.ShapeDtypeStruct((6, 128, width), BF16)] * count,
        compiler_params=params("pack"),
        name="pack",
    )(role, mixed, mixed, grad, grad, gated, gated, gain, gain, mean, inv)


def fold_slots(vg_ref, acc_ref, bands, last_band):
    for e in bands:
        at = (last_band - e) * PAIR
        for a in range(2):
            for b in range(2):
                slot = 2 * e + a - b
                if slot < 0 or slot >= BAND_BLOCKS or a == 1 and b == 1:
                    continue
                value = vg_ref[a * 128:(a + 1) * 128, at + b * 128:at + (b + 1) * 128]
                if a == b:
                    value = value + vg_ref[128:, at + 128:at + 256]
                rows = slice(slot * 128, (slot + 1) * 128)
                acc_ref[rows, :] = acc_ref[rows, :] + value


def local_body(role, m, g, u, n, mean_ref, inv_ref, v_ref, vt_ref, mo, no, acc, vg, a_s, d_s, bias):
    step = pl.program_id(0)

    @pl.when(step == 0)
    def _():
        vg[...] = jnp.zeros_like(vg)
        bias[...] = jnp.zeros_like(bias)
        acc[...] = jnp.zeros_like(acc)

    width = m.shape[1]
    for p in range(3):
        rows = slice(p * PAIR, (p + 1) * PAIR)
        hat = hat_of(m[rows, :], mean_ref[rows, :], inv_ref[rows, :])
        a_s[p] = (hat * n[...]).astype(BF16)
        d_s[p] = (g[rows, :].astype(F32) * u[rows, :].astype(F32)).astype(BF16)
    ones = jnp.ones((8, width), BF16)
    gain = jnp.zeros((1, width), F32)
    a_all = a_s[...].reshape(3 * PAIR, width)
    d_all = d_s[...].reshape(3 * PAIR, width)
    for p in range(3):
        rows = slice(p * PAIR, (p + 1) * PAIR)
        mixed = dot(v_ref[:, (2 - p) * PAIR:], a_all[:(p + 1) * PAIR])
        dnorm = dot(vt_ref[:, :(3 - p) * PAIR], d_all[p * PAIR:])
        at = (2 - p) * PAIR
        vg[:, at:] = vg[:, at:] + nt_dot(d_s[p], a_all[:(p + 1) * PAIR])
        mo[rows, :] = mixed.astype(BF16)
        no[rows, :] = dnorm.astype(BF16)
        gain = gain + jnp.sum(dnorm * a_s[p].astype(F32), axis=0, keepdims=True)
    bias[...] = bias[...] + nt_dot(ones, d_all)
    gain = gain / n[...]
    for k in range(width // 128):
        acc[pl.ds(SLOT_ROWS + step * (width // 128) + k, 1), :] = gain[:, k * 128:(k + 1) * 128]

    @pl.when(step == pl.num_programs(0) - 1)
    def _():
        fold_slots(vg, acc, range(3), 2)
        row = lax.broadcasted_iota(jnp.int32, (128, 128), 0)
        col = lax.broadcasted_iota(jnp.int32, (128, 128), 1)
        acc[:128, :] = jnp.where(row >= col, acc[:128, :], 0.0)
        for k in range(6):
            acc[pl.ds(SLOT_ROWS + GAIN_ROWS + role[0] * 6 + k, 1), :] = bias[0:1, k * 128:(k + 1) * 128]


def local_part(role, mixed, grad, gated, gain, mean, inv, v, vt):
    tokens, full = mixed.shape
    width = 512
    block = pl.BlockSpec((tokens, width), lambda j, r: (0, j))
    col = pl.BlockSpec((tokens, 128), lambda j, r: (0, 0))
    down = pl.BlockSpec((PAIR, 3 * PAIR), lambda j, r: (0, BANDS // 3 - 1))
    up = pl.BlockSpec((PAIR, 3 * PAIR), lambda j, r: (0, 0))
    return pl.pallas_call(
        local_body,
        grid_spec=pltpu.PrefetchScalarGridSpec(
            num_scalar_prefetch=1,
            grid=(full // width,),
            in_specs=[block, block, block, pl.BlockSpec((1, width), lambda j, r: (0, j)), col, col, down, up],
            out_specs=[block, block, pl.BlockSpec((ACC_ROWS, 128), lambda j, r: (0, 0))],
            scratch_shapes=[
                pltpu.VMEM((PAIR, 3 * PAIR), F32),
                pltpu.VMEM((3, PAIR, width), BF16),
                pltpu.VMEM((3, PAIR, width), BF16),
                pltpu.VMEM((8, tokens), F32),
            ],
        ),
        out_shape=[
            pltpu.HBM((tokens, full), BF16),
            pltpu.HBM((tokens, full), BF16),
            jax.ShapeDtypeStruct((ACC_ROWS, 128), F32),
        ],
        compiler_params=params("local"),
        name="local_part",
    )(role, mixed, grad, gated, gain, mean, inv, v, vt)


def owner_body(kind, width, first, second):
    mine = (0, 3) if kind == "z" else (1, 2)

    def body(role, cols, own, r0, r1, r2, gain_ref, v_in, vt_in, s_in, st_in, acc_in,
             o0, o1, o2, o3, acc_out,
             a_s, d_s, m_f, n_f, m_s, n_s, vg, sg, acc_s, v_ref, vt_ref, s_ref, st_ref, in_sem, acc_sem, m_sem, n_sem, t_sem):
        r = role[0]

        def third(buf, k):
            return buf.at[pl.ds(6 * k, 6)]

        mine_x, mine_y = own.at[0], own.at[1]
        if kind == "z":
            sources = {
                0: (mine_x, r0.at[0], r1.at[0], r0.at[1], r1.at[1], r2),
                3: (r2, r1.at[0], r0.at[0], r1.at[1], r0.at[1], mine_x),
            }
            targets = {
                0: ((o0.at[0], o1.at[0], o2), (o3, o0.at[1], o1.at[1])),
                3: ((o1.at[0], o0.at[0], o3), (o2, o1.at[1], o0.at[1])),
            }
        else:
            sources = {
                1: (r0, mine_x, r2.at[0], mine_y, r2.at[1], r1),
                2: (r1, r2.at[0], mine_x, r2.at[1], mine_y, r0),
            }
            targets = {
                1: ((o3.at[0], o2.at[0], o1), (o0, o3.at[1], o2.at[1])),
                2: ((o2.at[0], o3.at[0], o0), (o1, o2.at[1], o3.at[1])),
            }
        places = [third(a_s, 0), third(a_s, 1), third(a_s, 2), third(d_s, 0), third(d_s, 1), third(d_s, 2)]

        @pl.when((r == mine[0]) | (r == mine[1]))
        def _():
            fetch = pltpu.make_async_copy(acc_in, acc_s, acc_sem)
            fetch.start()
            for who in mine:
                @pl.when(r == who)
                def _():
                    copies = [
                        pltpu.make_async_copy(src, dst, in_sem.at[k])
                        for k, (src, dst) in enumerate(zip(sources[who], places))
                    ]
                    for copy in copies:
                        copy.start()
            loads = [
                pltpu.make_async_copy(src, dst, t_sem.at[k])
                for k, (src, dst) in enumerate(((v_in, v_ref), (vt_in, vt_ref), (s_in, s_ref), (st_in, st_ref)))
            ]
            for load in loads:
                load.start()
            vg[...] = jnp.zeros_like(vg)
            sg[...] = jnp.zeros_like(sg)
            m_f[:4] = jnp.zeros((4, 128, width), F32)
            n_f[...] = jnp.zeros_like(n_f)
            for k in range(6):
                pltpu.make_async_copy(mine_x, places[k], in_sem.at[k]).wait()
            for load in loads:
                load.wait()

            def pair(buf, p):
                return buf[pl.ds(2 * p, 2)].reshape(PAIR, width)

            def strided(i, carry):
                c0 = cols[BAND_BLOCKS + i, 0]
                c1 = cols[BAND_BLOCKS + i, 1]
                picked = jnp.concatenate([a_s[c0], a_s[c1]], axis=0)
                dmix = d_s[10 + i]
                m_f[4 + i] = dot(s_ref[...], picked)
                back = dot(st_ref[...], dmix)
                n_f[c0] = n_f[c0] + back[:128]
                n_f[c1] = n_f[c1] + back[128:]
                sg[...] = sg[...] + nt_dot(dmix, picked)
                return carry

            lax.fori_loop(0, 8, strided, 0)

            for dev in range(1, 4):
                low = 1 if dev == 3 else 0
                count = 3 * dev - low

                def forward(t, carry):
                    g = 3 * (dev - 1) + t
                    at = pl.ds(pl.multiple_of((BANDS - 1 - 3 * dev + low - t) * PAIR, PAIR), count * PAIR)
                    normed = a_s[2 * low:6 * dev].reshape(count * PAIR, width)
                    total = dot(v_ref[:, at], normed)
                    if dev > 1:
                        total = total + pair(m_f, g - 3)
                    m_s[pl.ds(2 * g, 2)] = total.astype(BF16).reshape(2, 128, width)
                    vg[:, at] = vg[:, at] + nt_dot(pair(d_s, g), normed)
                    return carry

                lax.fori_loop(0, 3, forward, 0)

            for who in mine:
                @pl.when(r == who)
                def _():
                    for k in range(3):
                        pltpu.make_async_copy(third(m_s, k), targets[who][0][k], m_sem.at[k]).start()

            total_gain = jnp.zeros((1, width), F32)
            for dev in range(3):
                count = 8 if dev == 0 else 9 - 3 * dev

                def backward(t, gain):
                    p = 3 * dev + t
                    at = pl.ds(pl.multiple_of((3 - t) * PAIR, PAIR), count * PAIR)
                    dmix = d_s[6 * dev:6 * dev + 2 * count].reshape(count * PAIR, width)
                    total = dot(vt_ref[:, at], dmix)
                    if dev < 2:
                        total = total + pair(n_f, p)
                    n_s[pl.ds(2 * p, 2)] = total.astype(BF16).reshape(2, 128, width)
                    return gain + jnp.sum(total * pair(a_s, p).astype(F32), axis=0, keepdims=True)

                total_gain = lax.fori_loop(0, 3, backward, total_gain)
            total_gain = total_gain / gain_ref[...]
            fetch.wait()
            base = jnp.where(r == mine[0], first, second) // 128
            for k in range(width // 128):
                where = pl.ds(SLOT_ROWS + base + k, 1)
                acc_s[where, :] = acc_s[where, :] + total_gain[:, k * 128:(k + 1) * 128]

            for who in mine:
                @pl.when(r == who)
                def _():
                    for k in range(3):
                        pltpu.make_async_copy(third(n_s, k), targets[who][1][k], n_sem.at[k]).start()

            fold_slots(vg, acc_s, range(1, 9), BANDS - 1)
            for s in range(NSTR):
                rows = slice((BAND_BLOCKS + s) * 128, (BAND_BLOCKS + s + 1) * 128)
                acc_s[rows, :] = acc_s[rows, :] + sg[:, s * 128:(s + 1) * 128]
            put = pltpu.make_async_copy(acc_s, acc_out, acc_sem)
            put.start()
            some = o2 if kind == "z" else o0
            for k in range(3):
                pltpu.make_async_copy(third(m_s, k), some, m_sem.at[k]).wait()
                pltpu.make_async_copy(third(n_s, k), some, n_sem.at[k]).wait()
            put.wait()

    return body


def owner(kind, first, second, width, role, cols, own, received, gain, tables, acc):
    hbm = pl.BlockSpec(memory_space=pl.ANY)
    v, vt, s, st = tables
    mine = (0, 3) if kind == "z" else (1, 2)

    def gain_at(i, r, c):
        return (0, jnp.where(r[0] == mine[1], second, first) // width)

    one = jax.ShapeDtypeStruct((6, 128, width), BF16)
    two = jax.ShapeDtypeStruct((2, 6, 128, width), BF16)
    return pl.pallas_call(
        owner_body(kind, width, first, second),
        grid_spec=pltpu.PrefetchScalarGridSpec(
            num_scalar_prefetch=2,
            grid=(1,),
            in_specs=[hbm] * 4
            + [pl.BlockSpec((1, width), gain_at)] + [hbm] * 5,
            out_specs=[hbm] * 5,
            scratch_shapes=[
                pltpu.VMEM((18, 128, width), BF16),
                pltpu.VMEM((18, 128, width), BF16),
                pltpu.VMEM((12, 128, width), F32),
                pltpu.VMEM((12, 128, width), F32),
                pltpu.VMEM((18, 128, width), BF16),
                pltpu.VMEM((18, 128, width), BF16),
                pltpu.VMEM((PAIR, BANDS * PAIR), F32),
                pltpu.VMEM((128, PAIR), F32),
                pltpu.VMEM((ACC_ROWS, 128), F32),
                pltpu.VMEM(v.shape, BF16),
                pltpu.VMEM(vt.shape, BF16),
                pltpu.VMEM(s.shape, BF16),
                pltpu.VMEM(st.shape, BF16),
                pltpu.SemaphoreType.DMA((6,)),
                pltpu.SemaphoreType.DMA,
                pltpu.SemaphoreType.DMA((3,)),
                pltpu.SemaphoreType.DMA((3,)),
                pltpu.SemaphoreType.DMA((4,)),
            ],
        ),
        out_shape=([two, two, one, one] if kind == "z" else [one, one, two, two])
        + [jax.ShapeDtypeStruct((ACC_ROWS, 128), F32)],
        input_output_aliases={11: 4},
        compiler_params=params("owner"),
    )(role, cols, own, *received, gain, v, vt, s, st, acc)


def absorb(first, second, width, role, mixed, grad, m_loc, n_loc, gain, mean, bias, pieces, carried, ends):
    tokens, full = mixed.shape
    begins = carried is None

    def at(j, r):
        return jnp.where((r[0] < 2) == (j == 0), first, second) // width

    def body(role, m, g, ml, nl, n, mean_ref, bias_ref, single_a, both_a, single_b, both_b, *rest):
        gated_out, grad_out, sums = rest[-3:]
        j = pl.program_id(0)
        r = role[0]
        edge = (r == 0) | (r == 3)

        @pl.when(j == 0)
        def _():
            sums[...] = jnp.zeros_like(sums) if begins else rest[2][...]

        def take(find):
            def group(i, carry):
                rows = some_rows(i)
                block, inside = i // 8, some_rows(i % 8)
                mean, bias = mean_ref[rows, :], bias_ref[rows, :]
                one, two = sums[0, rows, :], sums[1, rows, :]
                for lane in lanes_of(width):
                    off_m, off_n = find(block, inside, lane)
                    total = (off_m + ml[rows, lane].astype(F32) + bias).astype(BF16).astype(F32)
                    gated_out[rows, lane] = (g[rows, lane].astype(F32) * total).astype(BF16)
                    dnorm = (off_n + nl[rows, lane].astype(F32)).astype(BF16)
                    grad_out[rows, lane] = dnorm
                    hat_grad = dnorm.astype(F32) * n[:, lane]
                    one = one + hat_grad
                    two = two + hat_grad * (m[rows, lane].astype(F32) - mean)
                sums[0, rows, :] = one
                sums[1, rows, :] = two
                return carry

            lax.fori_loop(0, tokens // 16, group, 0)

        for half, single, both in ((j == 0, single_a, both_a), (j == 1, single_b, both_b)):
            @pl.when(half & edge)
            def _():
                def find(block, inside, lane):
                    one = single[block, inside, lane].astype(F32)
                    return jnp.where(r == 3, one, 0.0), jnp.where(r == 0, one, 0.0)

                take(find)

            @pl.when(half & jnp.logical_not(edge))
            def _():
                take(lambda block, inside, lane: (both[0, block, inside, lane].astype(F32), both[1, block, inside, lane].astype(F32)))

    block = pl.BlockSpec((tokens, width), lambda j, r: (0, at(j, r)))
    line = pl.BlockSpec((1, width), lambda j, r: (0, at(j, r)))
    col = pl.BlockSpec((tokens, 128), lambda j, r: (0, 0))
    one_a = one_b = pl.BlockSpec((6, 128, width), lambda j, r: (0, 0, 0), pipeline_mode=pl.Buffered(1))
    two_a = two_b = pl.BlockSpec((2, 6, 128, width), lambda j, r: (0, 0, 0, 0), pipeline_mode=pl.Buffered(1))
    hbm = pl.BlockSpec(memory_space=pl.ANY)
    total = pl.BlockSpec((2, tokens, 128), lambda j, r: (0, 0, 0))
    whole = jax.ShapeDtypeStruct((tokens, full), BF16) if ends else pltpu.HBM((tokens, full), BF16)
    return pl.pallas_call(
        body,
        grid_spec=pltpu.PrefetchScalarGridSpec(
            num_scalar_prefetch=1,
            grid=(2,),
            in_specs=[block] * 4 + [line, col, col, one_a, two_a, one_b, two_b] + ([] if begins else [hbm, hbm, total]),
            out_specs=[block, block, total],
        ),
        out_shape=[whole, whole, jax.ShapeDtypeStruct((2, tokens, 128), F32)],
        input_output_aliases={} if begins else {12: 0, 13: 1, 14: 2},
        compiler_params=params("absorb"),
    )(role, mixed, grad, m_loc, n_loc, gain, mean, bias, *pieces, *(carried or ()))


def finish_body(m, d, n, mean_ref, inv_ref, sums, value_out):
    rows, full = m.shape

    def group(i, carry):
        at = some_rows(i)
        inv, mean = inv_ref[at, :], mean_ref[at, :]
        shift = jnp.sum(sums[0, at, :], axis=1, keepdims=True) * (1.0 / full) * inv
        slope = jnp.sum(sums[1, at, :], axis=1, keepdims=True) * (1.0 / full) * inv * inv * inv
        for lane in lanes_of(full):
            value = d[at, lane].astype(F32) * n[:, lane] * inv - shift - (m[at, lane].astype(F32) - mean) * slope
            value_out[at, lane] = value.astype(BF16)
        return carry

    lax.fori_loop(0, rows // 16, group, 0)


def finish(mixed, dnorm, gain, mean, inv, sums):
    tokens, full = mixed.shape
    rows = 192
    row = pl.BlockSpec((rows, full), lambda i: (i, 0))
    col = pl.BlockSpec((rows, 128), lambda i: (i, 0))
    return pl.pallas_call(
        finish_body,
        grid=(tokens // rows,),
        in_specs=[row, row, pl.BlockSpec((1, full), lambda i: (0, 0)), col, col, pl.BlockSpec((2, rows, 128), lambda i: (0, i, 0))],
        out_specs=row,
        out_shape=jax.ShapeDtypeStruct((tokens, full), BF16),
        compiler_params=params("finish"),
        name="finish",
    )(mixed, dnorm, gain, mean, inv, sums)


def far_memory(*values):
    return tuple(pltpu.with_memory_space_constraint(x, pltpu.HBM) for x in values)


def move(value, pairs):
    return lax.ppermute(value, "seq", pairs)


def backwards(pairs):
    return tuple((b, a) for a, b in pairs)


def sum_over_all(acc):
    dp, seq = lax.axis_size("dp"), lax.axis_size("seq")

    def exchange(value, axis):
        return lax.all_to_all(value, axis, 0, 0, tiled=True)

    part = jnp.sum(exchange(acc.reshape(dp, -1, 128), "dp"), axis=0)
    part = exchange(jnp.broadcast_to(part, (seq,) + part.shape), "seq")
    part = jnp.sum(part, axis=0).astype(BF16)
    part = exchange(jnp.broadcast_to(part, (dp,) + part.shape), "dp").reshape(-1, 128)
    return part.astype(F32)


def shards_of_four(gated_part, mixed_part, out_grad, norm_gain, mix_bias, token_mixing_weight, stride_cols):
    return four(gated_part, mixed_part, out_grad, norm_gain, mix_bias, token_mixing_weight, stride_cols)


def four(gated_part, mixed_part, out_grad, norm_gain, mix_bias, token_mixing_weight, stride_cols):
    batch_size = lax.axis_size("dp")
    seq_parts = lax.axis_size("seq")
    gated, mixed, grad = far_memory(gated_part[0], mixed_part[0], out_grad[0])
    tokens, full = mixed.shape
    index = lax.axis_index("seq").astype(jnp.int32)
    role = index.reshape(1)
    gain = norm_gain.reshape(1, full)
    starts = segment_starts()
    mean, inv = stats(mixed)
    packed, received = {}, {}
    for key in ORDER:
        kind = key[0]
        packed[key] = pack(kind, role, mixed, grad, gated, gain, mean, inv, *starts[key])
        a, b, c = packed[key][:3]
        xs, ys, ds = X_PAIRS[kind], Y_PAIRS[kind], D_PAIRS[kind]
        if kind == "z":
            received[key] = (move(a, xs), move(b, ys), move(c, ds))
        else:
            received[key] = (move(packed[key][3], xs), move(c, ys), move(b, ds))
    tables = prep(token_mixing_weight)
    m_loc, n_loc, acc = local_part(role, mixed, grad, gated, gain, mean, inv, tables[0], tables[1])
    m_loc, n_loc = far_memory(m_loc, n_loc)
    back = {}
    for key in ORDER:
        kind = key[0]
        first, second, width = starts[key]
        *out, acc = owner(kind, first, second, width, role, stride_cols, far_memory(packed[key][0])[0], received[key], gain, tables, acc)
        xs, ys, ds = backwards(X_PAIRS[kind]), backwards(Y_PAIRS[kind]), D_PAIRS[kind]
        to_x = move(out[0], xs)
        to_y = move(out[1], ys)
        far = move(out[2], ds)
        own = far_memory(out[3])[0]
        back[key] = (own, to_x, far, to_y) if kind == "z" else (to_x, own, to_y, far)
    total = sum_over_all(acc)
    bias_col = lax.dynamic_slice_in_dim(mix_bias, index * tokens, tokens, 0)
    bias_col = jnp.broadcast_to(bias_col[:, None], (tokens, 128))
    carried = None
    for key in ORDER:
        kind = key[0]
        if carried is not None:
            carried = far_memory(*carried[:2]) + (carried[2],)
        carried = absorb(
            *starts[key], role, mixed, grad, m_loc, n_loc, gain, mean, bias_col, back[key], carried, key == ORDER[-1]
        )
    gated_grad, dnorm, sums = carried
    value_grad = finish(mixed, far_memory(dnorm)[0], gain, mean, inv, sums)
    total_len = tokens * seq_parts
    weight_grad = total[:SLOT_ROWS].reshape(18, 128, 128) / math.sqrt(batch_size * total_len * full)
    gain_grad = total[SLOT_ROWS:SLOT_ROWS + GAIN_ROWS].reshape(full) / math.sqrt(batch_size * total_len)
    bias_rows = lax.dynamic_slice_in_dim(total, SLOT_ROWS + GAIN_ROWS + index * 6, 6, 0).reshape(tokens)
    bias_grad = bias_rows / math.sqrt(batch_size * full)
    return (gated_grad[None], value_grad[None], weight_grad, gain_grad, bias_grad)


def solution(mesh):
    placed = (P("dp", "seq", None), P("dp", "seq", None), P("dp", "seq", None), P(), P(), P(), P())
    small = mesh.shape["seq"] == 4
    return jax.shard_map(
        shards_of_four if small else shards,
        mesh=mesh,
        in_specs=placed,
        out_specs=(P("dp", "seq", None), P("dp", "seq", None), P(), P(), P("seq")),
        check_vma=False,
    )
```
